32 devices in a mesh: ctx: 16 (over z, y, x), head: 2 (over core).
Axes of the slice: x: 2, y: 2, z: 4, core: 2. Of those that a mesh axis runs over, the one named last changes fastest.
Arguments:
- kv_cache: bfloat16 [2, 32768, 8, 256], P(None, 'ctx', 'head'), may hold values from -12 to 12
- keep_rows: int32 [2, 128, 128], P(None, 'ctx'), may hold values from 0 to 256, as said below
- block_target: int32 [2, 128, 2], P(None, 'ctx'), may hold values from 0 to 15, as said below
- future_queries: bfloat16 [2, 256, 8192], P(None, 'ctx', 'head'), may hold values from -32 to 32
- new_tokens: bfloat16 [4, 2, 8192], P(None, None, 'ctx'), may hold values from -6 to 6
- w_query: bfloat16 [8192, 8192], P('ctx', 'head'), may hold values from -16 to 16
- w_keyval: bfloat16 [8192, 8, 256], P('ctx', 'head'), may hold values from -0.25 to 0.25
- w_out: bfloat16 [8192, 8192], P('head', 'ctx'), may hold values from -0.1875 to 0.1875
Outputs:
- packed_cache: bfloat16 [2, 16384, 8, 256], P(None, 'ctx', 'head')
- packed_scores: float32 [2, 8, 16384], P(None, 'head', 'ctx')
- decoded: bfloat16 [4, 2, 8192], P(None, None, 'ctx')
The draws below stay inside these ranges and needn't reach their ends.
Inputs may be any that keep to these rules, and one draw needn't show every extreme that they name: `keep_rows`: in each list the kept offsets come first, distinct and increasing, then entries equal to 256 mark none; every list holds at least one kept offset, and in each request some list holds 128. `block_target`: entry 0 is the destination device, entry 1 the destination block slot. Both depend only on the request and on the list's place b among the 8 lists of its device: the device is (source device + d) modulo 16, where the 16 values of d are 0 to 15, each once; within a request the slots are a permutation of 0 to 7.
All inputs are finite; a program needn't handle non-finite values.
Results may differ from the reference program's by a relative error of at most 0.007.
The reference program's roundings to bfloat16 on the way count: a program that leaves them out, or rounds other values in their place, can miss the bound.
Values may be sent and summed in bfloat16 or wider, within the bound.
No kernel may reach another device: no remote copies, remote signals or barrier semaphores. Data moves between devices by JAX's collectives and lax.ppermute only.
A program may use at most 128 MiB of HBM per device.

```python
import math
import jax
import jax.numpy as jnp
from jax import lax

D = 8192
H = 64
KVH = 8
HD = 128
G = 8
REQ = 2
BLK = 128
LB = 8
SEQ = 32768
SLOTS = 16384
QS = 256
STEPS = 4
N_CTX = 16


def draw_keep_rows(key, part):
    first, second, third = jax.random.split(key, 3)
    span = 2 * BLK
    counts = jax.random.randint(first, (REQ, N_CTX * LB), 1, BLK + 1)
    chosen = jax.random.randint(second, (REQ,), 0, N_CTX * LB)
    counts = jnp.where(jnp.arange(N_CTX * LB)[None, :] == chosen[:, None], BLK, counts)
    noise = jax.random.randint(third, (REQ, N_CTX * LB, span), 0, 1 << 20)
    distinct = noise * span + jnp.arange(span)[None, None, :]
    order = jnp.argsort(distinct, axis=-1)
    ranks = jnp.argsort(order, axis=-1)
    kept = ranks < counts[:, :, None]
    offsets = jnp.arange(span)[None, None, :]
    sortkey = jnp.where(kept, offsets, span + offsets)
    listed = jnp.argsort(sortkey, axis=-1)[:, :, :BLK]
    places = jnp.arange(BLK)[None, None, :]
    return jnp.where(places < counts[:, :, None], listed, span).astype(jnp.int32)


def slot_order(subkey):
    return jax.random.permutation(subkey, LB)


def draw_block_target(key, part):
    first, second = jax.random.split(key)
    pairs = REQ * LB
    shuffled = jax.random.permutation(first, pairs)
    offsets = shuffled * N_CTX // pairs
    if 2 * pairs <= N_CTX:
        offsets = jnp.where(shuffled == 0, 1, offsets)
    offsets = offsets.reshape(REQ, LB)
    slot_keys = jax.random.split(second, REQ)
    slots = jax.vmap(slot_order)(slot_keys)
    source = jnp.arange(N_CTX * LB) // LB
    device = (source[None, :] + jnp.tile(offsets, (1, N_CTX))) % N_CTX
    slot_all = jnp.tile(slots, (1, N_CTX))
    return jnp.stack([device, slot_all], axis=-1).astype(jnp.int32)


def draw_future_queries(key, part):
    first, second, third = jax.random.split(key, 3)
    centre = 0.5 * jax.random.normal(first, (1, 1, H, HD))
    spread = jnp.clip(jax.random.normal(second, (REQ, QS, H, HD)), -4.0, 4.0)
    scales = jnp.exp(jax.random.uniform(third, (REQ, QS, 1, 1), minval=-0.7, maxval=0.7))
    values = jnp.clip(centre + spread * scales, -32.0, 32.0)
    return values.reshape(REQ, QS, H * HD).astype(jnp.bfloat16)


def draw_w_query(key, part):
    first, second, third = jax.random.split(key, 3)
    base = jnp.clip(jax.random.normal(first, (D, H, HD)), -4.0, 4.0)
    powers = jax.random.randint(second, (H,), 0, 6)
    picked = jax.random.permutation(third, H)
    heads = jnp.arange(H)
    powers = jnp.where(heads == picked[0], 5, powers)
    powers = jnp.where(heads == picked[1], 0, powers)
    strength = jnp.power(2.0, powers.astype(jnp.float32))
    values = base * strength[None, :, None] / math.sqrt(D)
    return values.reshape(D, H * HD).astype(jnp.bfloat16)


def levels(stream_key, dims, cuts, smallest, high):
    gain, own = 1.0, jax.random.fold_in(stream_key, 6)
    for axis_at, parts in cuts:
        steps = jnp.exp(jax.random.uniform(jax.random.fold_in(own, axis_at), (parts,), jnp.float32, smallest / len(cuts), high / len(cuts)))
        gain = gain * jnp.repeat(steps, dims[axis_at] // parts).reshape([-1 if axis == axis_at else 1 for axis in range(len(dims))])
    return gain


def normal_values(rng, dims, scale, most, cuts=(), held_as=jnp.bfloat16):
    level = levels(rng, dims, cuts, -0.22, 0.18) if cuts else 1.0
    entries = jax.random.normal(rng, dims, jnp.float32) * scale * level
    return jnp.minimum(jnp.maximum(entries, -most), most).astype(held_as)


def setup_inputs(seed: int = 0) -> dict:
    key_list = jax.random.split(jax.random.key(seed), 9)
    return {
        "kv_cache": normal_values(key_list[0], (REQ, SEQ, KVH, 2 * HD), 2.0, 12.0, ((1, 16), (2, 2))),
        "keep_rows": draw_keep_rows(jax.random.fold_in(key_list[8], 71), 0),
        "block_target": draw_block_target(jax.random.fold_in(key_list[8], 71), 0),
        "future_queries": draw_future_queries(jax.random.fold_in(key_list[8], 71), 0),
        "new_tokens": normal_values(key_list[4], (STEPS, REQ, D), 1.0, 6.0, ((2, 16),)),
        "w_query": draw_w_query(jax.random.fold_in(key_list[8], 71), 0),
        "w_keyval": normal_values(key_list[6], (D, KVH, 2 * HD), (D // 16) ** -0.5, 0.25, ((0, 16), (1, 2))),
        "w_out": normal_values(key_list[7], (H * HD, D), (G * HD) ** -0.5, 0.1875, ((0, 2), (1, 16))),
    }


HIGHEST = lax.Precision.HIGHEST
EPSILON = 1e-05

def head_scores(keys, mean_q, cov_q):
    lifted = keys.astype(jnp.float32)
    linear = jnp.einsum('nd,gd->ng', lifted, mean_q, precision=HIGHEST)
    turned = jnp.einsum('nd,gde->nge', lifted, cov_q, precision=HIGHEST)
    quadratic = lax.optimization_barrier(jnp.sum(turned * lifted[:, None, :], axis=-1))
    logits = linear / math.sqrt(HD) + quadratic / (2.0 * HD)
    top = lax.optimization_barrier(jnp.max(logits, axis=1))
    return top + jnp.log(lax.optimization_barrier(jnp.mean(jnp.exp(logits - top[:, None]), axis=1)))

def reference(kv_cache, keep_rows, block_target, future_queries, new_tokens, w_query, w_keyval, w_out):
    group = H // KVH
    span = 2 * BLK
    lists = N_CTX * LB
    sampled = future_queries.astype(jnp.float32).reshape(REQ, QS, H, HD)
    mean_q = lax.optimization_barrier(jnp.sum(sampled, axis=1)) / QS
    second = jnp.einsum('rshd,rshe->rhde', sampled, sampled, precision=HIGHEST)
    cov_q = second / QS - mean_q[:, :, :, None] * mean_q[:, :, None, :]
    spans = kv_cache.reshape(REQ, lists, span, KVH, 2 * HD)
    padded = jnp.concatenate([spans, jnp.zeros((REQ, lists, 1, KVH, 2 * HD), kv_cache.dtype)], axis=2)
    picked = jnp.take_along_axis(padded, keep_rows[:, :, :, None, None], axis=2)
    counts = lax.optimization_barrier(jnp.sum((keep_rows < span).astype(jnp.int32), axis=-1))
    target = (block_target[:, :, 0] * LB + block_target[:, :, 1]).astype(jnp.int32)
    request_index = jnp.arange(REQ, dtype=jnp.int32)[:, None]
    packed_blocks = jnp.zeros_like(picked).at[request_index, target].set(picked)
    packed_cache = packed_blocks.reshape(REQ, SLOTS, KVH, 2 * HD)
    placed_counts = jnp.zeros((REQ, lists), jnp.int32).at[request_index, target].set(counts)
    live = (jnp.arange(BLK, dtype=jnp.int32)[None, None, :] < placed_counts[:, :, None]).reshape(REQ, SLOTS)
    score_rows = []
    for request in range(REQ):
        per_head = []
        for head in range(KVH):
            per_head.append(head_scores(packed_cache[request, :, head, :HD], mean_q[request, head * group:(head + 1) * group], cov_q[request, head * group:(head + 1) * group]))
        score_rows.append(jnp.stack(per_head, axis=0))
    packed_scores = jnp.stack(score_rows, axis=0)
    flat = new_tokens.reshape(STEPS * REQ, D)
    wide = flat.astype(jnp.float32)
    inverse = lax.rsqrt(lax.optimization_barrier(jnp.sum(wide * wide, axis=-1)) / D + EPSILON)
    query = (jnp.dot(flat, w_query, preferred_element_type=jnp.float32) * inverse[:, None]).astype(jnp.bfloat16)
    fresh = (jnp.dot(flat, w_keyval.reshape(D, KVH * 2 * HD), preferred_element_type=jnp.float32) * inverse[:, None]).astype(jnp.bfloat16)
    query = query.reshape(STEPS, REQ, KVH, group, HD)
    fresh = fresh.reshape(STEPS, REQ, KVH, 2 * HD)
    step_of_row = jnp.arange(STEPS * group, dtype=jnp.int32) // group
    causal = step_of_row[:, None] >= jnp.arange(STEPS, dtype=jnp.int32)[None, :]
    outputs = []
    for request in range(REQ):
        heads_out = []
        for head in range(KVH):
            rows_q = query[:, request, head].reshape(STEPS * group, HD)
            cached = packed_cache[request, :, head]
            recent = fresh[:, request, head]
            logit_cache = jnp.dot(rows_q, cached[:, :HD].T, preferred_element_type=jnp.float32) / math.sqrt(HD)
            logit_cache = jnp.where(live[request][None, :], logit_cache, -jnp.inf)
            logit_new = jnp.dot(rows_q, recent[:, :HD].T, preferred_element_type=jnp.float32) / math.sqrt(HD)
            logit_new = jnp.where(causal, logit_new, -jnp.inf)
            top = jnp.maximum(lax.optimization_barrier(jnp.max(logit_cache, axis=1)), lax.optimization_barrier(jnp.max(logit_new, axis=1)))
            weight_cache = jnp.exp(logit_cache - top[:, None])
            weight_new = jnp.exp(logit_new - top[:, None])
            total = lax.optimization_barrier(jnp.sum(weight_cache, axis=1)) + lax.optimization_barrier(jnp.sum(weight_new, axis=1))
            weighted = jnp.dot(weight_cache.astype(jnp.bfloat16), cached[:, HD:], preferred_element_type=jnp.float32)
            weighted = weighted + jnp.dot(weight_new.astype(jnp.bfloat16), recent[:, HD:], preferred_element_type=jnp.float32)
            heads_out.append((weighted / total[:, None]).astype(jnp.bfloat16).reshape(STEPS, group * HD))
        outputs.append(jnp.concatenate(heads_out, axis=1))
    attended = jnp.stack(outputs, axis=1).reshape(STEPS * REQ, H * HD)
    decoded = jnp.dot(attended, w_out, preferred_element_type=jnp.float32).astype(jnp.bfloat16).reshape(STEPS, REQ, D)
    return (packed_cache, packed_scores, decoded)
```

```python
import math

import jax
import jax.numpy as jnp
from jax import lax
from jax.experimental import pallas as pl
from jax.experimental.pallas import tpu as pltpu
from jax.sharding import PartitionSpec as P

D = 8192
H = 64
QS = 256
EPSILON = 1e-05
HIGHEST = lax.Precision.HIGHEST
BF = jnp.bfloat16
F32 = jnp.float32
STAT = 144
LARGE = 1e30
VMEM_LIMIT = 48 << 20
ANY = pl.BlockSpec(memory_space=pl.ANY)
SMEM = pl.BlockSpec(memory_space=pltpu.SMEM)
VMEM = pl.BlockSpec(memory_space=pltpu.VMEM)
NT = (((1,), (1,)), ((), ()))
TN = (((0,), (0,)), ((), ()))


def params():
    return pltpu.CompilerParams(vmem_limit_bytes=VMEM_LIMIT)


def pack_kernel(keep, target, kv, send, spans, blocks, in_sem, out_sem):
    items, width = keep.shape
    span = 2 * width
    lists = items // kv.shape[0]

    def fetch(m):
        return pltpu.make_async_copy(
            kv.at[m // lists, pl.ds((m % lists) * span, span)], spans.at[m, pl.ds(0, span)], in_sem.at[m]
        )

    def put(m):
        return pltpu.make_async_copy(blocks.at[m], send.at[target[m, 0]], out_sem.at[m])

    for m in range(items):
        fetch(m).start()
        spans[m, span] = jnp.zeros(spans.shape[2:], spans.dtype)

    def one(m, carry):
        fetch(m).wait()

        def rows(j, inner):
            for u in range(16):
                at = j * 16 + u
                blocks[m, at] = spans[m, keep[m, at]]
            return inner

        lax.fori_loop(0, width // 16, rows, 0)
        put(m).start()
        return carry

    lax.fori_loop(0, items, one, 0)
    for m in range(items):
        put(m).wait()


def pack(kv_cache, keep, target):
    items, width = keep.shape
    tail = kv_cache.shape[2:]
    return pl.pallas_call(
        pack_kernel,
        out_shape=jax.ShapeDtypeStruct((items, width, *tail), kv_cache.dtype),
        in_specs=[SMEM, SMEM, ANY],
        out_specs=ANY,
        scratch_shapes=[
            pltpu.VMEM((items, 2 * width + 8, *tail), kv_cache.dtype),
            pltpu.VMEM((items, width, *tail), kv_cache.dtype),
            pltpu.SemaphoreType.DMA((items,)),
            pltpu.SemaphoreType.DMA((items,)),
        ],
        compiler_params=params(),
        name="pack_rows",
    )(keep, target, kv_cache)


def project_kernel(tokens, wq, wkv, out):
    i = pl.program_id(0)
    x = tokens[...]
    part = jnp.dot(x, wq[...], preferred_element_type=F32)
    for r in range(2):
        for g in range(8):
            out[r * 8 + i * 2 + g // 4, (g % 4) * 4 : (g % 4) * 4 + 4, :] = part[
                r * 4 : r * 4 + 4, g * 128 : g * 128 + 128
            ]

    @pl.when(i == 0)
    def _():
        heads = pltpu.einshape("nhd->hnd", wkv[...])
        wide = x.astype(F32)
        squares = jnp.sum(wide * wide, axis=1, keepdims=True)
        row = lax.broadcasted_iota(jnp.int32, (8, 128), 0)
        lane = lax.broadcasted_iota(jnp.int32, (8, 128), 1)
        line = jnp.sum(jnp.where(row == lane, squares, 0.0), axis=0, keepdims=True)
        line = jnp.concatenate([line, jnp.zeros((3, 128), F32)], axis=0)
        for p in range(16):
            out[p, 20:24, :] = line
        for j in range(4):
            pair = jnp.dot(x, heads[j], preferred_element_type=F32)
            for r in range(2):
                for half in range(2):
                    out[r * 8 + j * 2 + half, 16:20, :] = pair[
                        r * 4 : r * 4 + 4, half * 128 : half * 128 + 128
                    ]


def project(tokens, w_query, w_keyval):
    depth, columns = w_query.shape
    step = columns // 4
    return pl.pallas_call(
        project_kernel,
        out_shape=jax.ShapeDtypeStruct((16, 24, 128), F32),
        grid=(4,),
        in_specs=[
            pl.BlockSpec((8, depth), lambda i: (0, 0)),
            pl.BlockSpec((depth, step), lambda i: (0, i)),
            pl.BlockSpec(w_keyval.shape, lambda i: (0, 0, 0)),
        ],
        out_specs=pl.BlockSpec((16, 24, 128), lambda i: (0, 0, 0)),
        compiler_params=params(),
        name="project_tokens",
    )(tokens, w_query, w_keyval)


def normalize_kernel(place, parts, out):
    total = jnp.sum(parts[...], axis=0)
    request = place[0] // 8
    row = lax.broadcasted_iota(jnp.int32, (24, 128), 0)
    lane = lax.broadcasted_iota(jnp.int32, (24, 128), 1)
    squares = jnp.where(lane == request * 4 + row % 4, total[20:21, :], 0.0)
    inverse = lax.rsqrt(jnp.sum(squares, axis=1, keepdims=True) / D + EPSILON)
    scaled = jnp.where(row < 20, total * inverse, 0.0)
    rounded = jnp.concatenate([scaled, jnp.zeros((8, 128), F32)], axis=0).astype(BF)
    out[...] = jnp.broadcast_to(rounded[None], out.shape)


def normalize(place, parts):
    return pl.pallas_call(
        normalize_kernel,
        out_shape=jax.ShapeDtypeStruct((16, 32, 128), BF),
        in_specs=[SMEM, VMEM],
        out_specs=VMEM,
        compiler_params=params(),
        name="normalize_tokens",
    )(place, parts)


def attend_kernel(target, query, bias, send, out, rows, logits, sem):
    items = rows.shape[0]
    width = rows.shape[1]
    wide = width * 4

    def fetch(m):
        return pltpu.make_async_copy(send.at[target[m, 0]], rows.at[m], sem.at[m])

    for m in range(items):
        fetch(m).start()
    head = lax.broadcasted_iota(jnp.int32, (128, wide), 0) // 32
    lane = lax.broadcasted_iota(jnp.int32, (128, wide), 1) % 4
    own = head == lane
    for r in range(2):
        q = query[r * 8 : r * 8 + 8, 0:16, :].reshape(128, 128)
        for b in range(8):
            m = r * 8 + b
            fetch(m).wait()
            keys = rows[m, :, :, 0:128].reshape(wide, 128)
            scores = lax.dot_general(q, keys, NT, preferred_element_type=F32) / math.sqrt(128)
            scores = jnp.where(own, scores, -LARGE) + bias[m : m + 1, :]
            logits[:, b * wide : b * wide + wide] = scores
        top = jnp.max(logits[...], axis=1, keepdims=True)
        total = jnp.zeros((128, 1), F32)
        weighted = jnp.zeros((128, 128), F32)
        for b in range(8):
            weights = jnp.exp(logits[:, b * wide : b * wide + wide] - top)
            total = total + jnp.sum(weights, axis=1, keepdims=True)
            values = rows[r * 8 + b, :, :, 128:256].reshape(wide, 128)
            weighted = weighted + jnp.dot(weights.astype(BF), values, preferred_element_type=F32)
        top_line = jnp.broadcast_to(top, (128, 128)).T[0:1, :]
        total_line = jnp.broadcast_to(total, (128, 128)).T[0:1, :]
        lines = jnp.concatenate([top_line, total_line, jnp.zeros((6, 128), F32)], axis=0)
        for i in range(8):
            out[r * 8 + i, 0:16, :] = weighted[i * 16 : i * 16 + 16, :]
            out[r * 8 + i, 16:24, :] = lines


def attend(target, query, bias, send):
    items, width = send.shape[:2]
    return pl.pallas_call(
        attend_kernel,
        out_shape=jax.ShapeDtypeStruct((16, 24, 128), F32),
        in_specs=[SMEM, VMEM, VMEM, ANY],
        out_specs=VMEM,
        scratch_shapes=[
            pltpu.VMEM(send.shape, send.dtype),
            pltpu.VMEM((128, 8 * width * 4), F32),
            pltpu.SemaphoreType.DMA((items,)),
        ],
        compiler_params=params(),
        name="attend_kept",
    )(target, query, bias, send)


def combine_kernel(place, parts, query, out):
    p = place[0]
    mine = query[p, 0:16, :]
    pair = (p // 2) * 2
    fresh_key = query[pair, 16:32, :]
    fresh_value = query[pair + 1, 16:32, :]
    recent = lax.dot_general(mine, fresh_key, NT, preferred_element_type=F32) / math.sqrt(128)
    step = lax.broadcasted_iota(jnp.int32, (16, 16), 0) % 4
    column = lax.broadcasted_iota(jnp.int32, (16, 16), 1)
    recent = jnp.where(column <= step, recent, -LARGE)
    row = lax.broadcasted_iota(jnp.int32, (16, 128), 0)
    lane = lax.broadcasted_iota(jnp.int32, (16, 128), 1)
    chosen = lane == (p % 8) * 16 + row
    tops, totals = [], []
    for s in range(16):
        tops.append(jnp.sum(jnp.where(chosen, parts[s, 16:17, :], 0.0), axis=1, keepdims=True))
        totals.append(jnp.sum(jnp.where(chosen, parts[s, 17:18, :], 0.0), axis=1, keepdims=True))
    best = jnp.max(recent, axis=1, keepdims=True)
    for s in range(16):
        best = jnp.maximum(best, tops[s])
    weights = jnp.exp(recent - best)
    total = jnp.sum(weights, axis=1, keepdims=True)
    weighted = jnp.dot(weights.astype(BF), fresh_value, preferred_element_type=F32)
    for s in range(16):
        factor = jnp.exp(tops[s] - best)
        total = total + totals[s] * factor
        weighted = weighted + parts[s, 0:16, :] * factor
    out[...] = jnp.broadcast_to((weighted / total).astype(BF)[None], out.shape)


def combine(place, parts, query):
    return pl.pallas_call(
        combine_kernel,
        out_shape=jax.ShapeDtypeStruct((16, 16, 128), BF),
        in_specs=[SMEM, VMEM, VMEM],
        out_specs=VMEM,
        compiler_params=params(),
        name="combine_parts",
    )(place, parts, query)


def moments_kernel(samples, out):
    for i in range(4):
        q = samples[:, i * 128 : i * 128 + 128]
        second = lax.dot_general(q, q, TN, preferred_element_type=F32)
        mean = jnp.sum(q.astype(F32), axis=0, keepdims=True) / QS
        first = jnp.concatenate([mean, jnp.zeros((7, 128), F32)], axis=0)
        outer = lax.dot_general(first, first, TN, preferred_element_type=F32, precision=HIGHEST)
        cov = second / QS - outer
        scaled = mean / math.sqrt(128)
        high = scaled.astype(BF).astype(F32)
        low = scaled - high
        lines = jnp.concatenate([high, low, jnp.zeros((14, 128), F32)], axis=0)
        out[i, 0:128, :] = cov.astype(BF)
        out[i, 128:144, :] = lines.astype(BF)


def head_moments(samples):
    return pl.pallas_call(
        moments_kernel,
        out_shape=jax.ShapeDtypeStruct((4, STAT, 128), BF),
        in_specs=[VMEM],
        out_specs=VMEM,
        compiler_params=params(),
        name="moments",
    )(samples)


def reverse_bits(value, order):
    place = 0
    for at, bit in enumerate(order):
        place = place + ((value // bit) % 2) * (1 << at)
    return place


def score_kernel(orders, place, target, arrived, stat_a, stat_b, packed, scores, blocks, stats, in_sem, out_sem, a_sem, b_sem):
    items = blocks.shape[0]
    lists = items // 2
    me = place[0]

    def at(m):
        return (m // lists) * lists + target[m, 1]

    def fetch(m):
        source = (2 * me - target[m, 0] + 16) % 16
        return pltpu.make_async_copy(arrived.at[source], blocks.at[at(m)], in_sem.at[m])

    def put(m):
        return pltpu.make_async_copy(blocks.at[m], packed.at[m], out_sem.at[m])

    def take(o, half, stat, sem):
        index = reverse_bits(jnp.bitwise_xor(me, o), orders[half])
        return pltpu.make_async_copy(stat.at[index], stats.at[o, pl.ds(half * 2, 2)], sem.at[o])

    for m in range(items):
        fetch(m).start()
    for o in range(16):
        take(o, 0, stat_a, a_sem).start()
        take(o, 1, stat_b, b_sem).start()
    for m in range(items):
        fetch(m).wait()
    for m in range(items):
        put(m).start()
    for o in range(16):
        take(o, 0, stat_a, a_sem).wait()
        take(o, 1, stat_b, b_sem).wait()
    for r in range(2):
        for j in range(4):
            first = r * 8 + j * 2
            table = stats[first : first + 2].reshape(8 * STAT, 128)
            for c in range(4):
                keys = blocks[r * 8 + c * 2 : r * 8 + c * 2 + 2, :, j, 0:128].reshape(256, 128)
                turned = lax.dot_general(table, keys, NT, preferred_element_type=F32)
                flipped = keys.astype(F32).T
                lines = []
                for g in range(8):
                    base = g * STAT
                    quadratic = jnp.sum(turned[base : base + 128] * flipped, axis=0, keepdims=True)
                    linear = turned[base + 128 : base + 129] + turned[base + 129 : base + 130]
                    lines.append(linear + quadratic / 256.0)
                logit = jnp.concatenate(lines, axis=0)
                top = jnp.max(logit, axis=0, keepdims=True)
                mean = jnp.sum(jnp.exp(logit - top), axis=0, keepdims=True) / 8.0
                scores[r, j : j + 1, c * 256 : c * 256 + 256] = top + jnp.log(mean)
    for m in range(items):
        put(m).wait()


def score(orders, place, target, arrived, stat_a, stat_b):
    items, width = arrived.shape[:2]

    def kernel(*refs):
        score_kernel(orders, *refs)

    return pl.pallas_call(
        kernel,
        out_shape=(
            jax.ShapeDtypeStruct(arrived.shape, arrived.dtype),
            jax.ShapeDtypeStruct((2, 4, items // 2 * width), F32),
        ),
        in_specs=[SMEM, SMEM, ANY, ANY, ANY],
        out_specs=(ANY, VMEM),
        scratch_shapes=[
            pltpu.VMEM(arrived.shape, arrived.dtype),
            pltpu.VMEM((16, 4, STAT, 128), BF),
            pltpu.SemaphoreType.DMA((items,)),
            pltpu.SemaphoreType.DMA((items,)),
            pltpu.SemaphoreType.DMA((16,)),
            pltpu.SemaphoreType.DMA((16,)),
        ],
        compiler_params=params(),
        name="place_and_score",
    )(place, target, arrived, stat_a, stat_b)


def exchange(value):
    return lax.all_to_all(value, "ctx", split_axis=0, concat_axis=0, tiled=True)


def doubled(value, order):
    value = value[None]
    for bit in order:
        pairs = [(i, i ^ bit) for i in range(16)]
        value = jnp.concatenate([value, lax.ppermute(value, "ctx", pairs)], axis=0)
    return value


def sixteen(
    kv_cache, keep_rows, block_target, future_queries, new_tokens, w_query, w_keyval, w_out
):
    requests, cache_rows, local_kv, pair = kv_cache.shape
    lists, width = keep_rows.shape[1:]
    items = requests * lists
    keep = keep_rows.reshape(items, width)
    target = block_target.reshape(items, 2)
    place = lax.axis_index("ctx").astype(jnp.int32).reshape(1)
    tokens = jnp.transpose(new_tokens, (1, 0, 2)).reshape(8, new_tokens.shape[2])
    samples = future_queries.reshape(2, 16, 8, 512)
    samples = jnp.transpose(samples, (0, 2, 1, 3)).reshape(16, 16, 512)
    samples = exchange(samples).reshape(256, 512)
    parts = exchange(project(tokens, w_query, w_keyval))
    send = pack(kv_cache, keep, target)
    bias = jnp.where(keep < 2 * width, 0.0, -LARGE).astype(F32)
    bias = jnp.broadcast_to(bias[:, :, None], (items, width, 4)).reshape(items, width * 4)
    query = exchange(normalize(place, parts))
    stat = head_moments(samples)
    orders = ((8, 4, 2, 1), (8, 4, 1, 2))
    stat_a = doubled(stat[:2], orders[0])
    stat_b = doubled(stat[2:], orders[1])
    joined = exchange(attend(target, query, bias, send))
    attended = exchange(combine(place, joined, query))
    send, attended = lax.optimization_barrier((send, attended))
    arrived = exchange(send)
    packed, scores = score(orders, place, target, arrived, stat_a, stat_b)
    rows = attended.reshape(requests, 32, 4, 128)
    rows = jnp.transpose(rows, (2, 0, 1, 3)).reshape(8, 4096)
    partial_value = jnp.dot(rows, w_out, preferred_element_type=F32)
    decoded = lax.psum(partial_value, "head").astype(BF).reshape(4, requests, w_out.shape[1])
    return packed.reshape(requests, lists * width, local_kv, pair), scores, decoded
def joined(value, axis, join):
    pieces = jax.tree.map(lambda part: lax.all_gather(part, axis), value)
    head = jax.tree.map(lambda part: part[0], pieces)
    tail = jax.tree.map(lambda part: part[1:], pieces)
    running, _ = lax.scan(lambda running, share: (join(running, share), None), head, tail)
    return running


def group_scores(keys, mean_q, cov_q):
    lifted = keys.astype(jnp.float32)
    linear = jnp.einsum("nkd,kgd->nkg", lifted, mean_q, precision=HIGHEST)
    turned = jnp.einsum("nkd,kgde->nkge", lifted, cov_q, precision=HIGHEST)
    quadratic = jnp.sum(turned * lifted[:, :, None, :], axis=-1)
    logits = linear / math.sqrt(keys.shape[-1]) + quadratic / (2.0 * keys.shape[-1])
    top = jnp.max(logits, axis=2)
    return top + jnp.log(jnp.mean(jnp.exp(logits - top[:, :, None]), axis=2))


def combine_parts(first, second):
    top_a, total_a, weighted_a = first
    top_b, total_b, weighted_b = second
    best = jnp.maximum(top_a, top_b)
    factor_a = jnp.exp(top_a - best)
    factor_b = jnp.exp(top_b - best)
    return (
        best,
        total_a * factor_a + total_b * factor_b,
        weighted_a * factor_a[..., None] + weighted_b * factor_b[..., None],
    )


def moments(sample):
    second = jnp.einsum("rshd,rshe->rhde", sample, sample, preferred_element_type=jnp.float32)
    summed = jnp.sum(sample.astype(jnp.float32), axis=1)
    return (second, summed)


KVH = 8


def per_device(
    kv_cache, keep_rows, block_target, future_queries, new_tokens, w_query, w_keyval, w_out
):
    requests, cache_rows, local_kv, pair = kv_cache.shape
    head_size = pair // 2
    lists, width = (keep_rows.shape[1], keep_rows.shape[2])
    span = 2 * width
    group = H // KVH
    ctx_count = lax.axis_size("ctx")
    position = lax.axis_index("ctx")
    root_size = math.sqrt(head_size)
    sample = future_queries.reshape(requests, -1, local_kv * group, head_size)
    second, summed = moments(sample)
    second, summed = lax.psum((second, summed), "ctx")
    mean_q = summed / QS
    cov_q = second / QS - mean_q[..., :, None] * mean_q[..., None, :]
    mean_q = mean_q.reshape(requests, local_kv, group, head_size)
    cov_q = cov_q.reshape(requests, local_kv, group, head_size, head_size)
    span_index = jnp.arange(span, dtype=jnp.int32)
    block_kv, block_score, block_count = ([], [], [])
    for request in range(requests):
        listed = keep_rows[request]
        picker = (listed[:, :, None] == span_index[None, None, :]).astype(jnp.bfloat16)
        spans = kv_cache[request].reshape(lists, span, local_kv * pair)
        chosen = jnp.einsum(
            "bjs,bsc->bjc", picker, spans, preferred_element_type=jnp.float32
        ).astype(jnp.bfloat16)
        chosen = chosen.reshape(lists, width, local_kv, pair)
        every = group_scores(kv_cache[request][:, :, :head_size], mean_q[request], cov_q[request])
        every = every.reshape(lists, span, local_kv)
        picked = jnp.einsum("bjs,bsk->bkj", picker.astype(jnp.float32), every, precision=HIGHEST)
        block_kv.append(chosen)
        block_score.append(picked)
        block_count.append(jnp.sum((listed < span).astype(jnp.int32), axis=1))
    items_kv = jnp.concatenate(block_kv, axis=0)
    items_score = jnp.concatenate(block_score, axis=0)
    items_count = jnp.concatenate(block_count, axis=0)
    total_items = requests * lists
    targets = block_target.reshape(total_items, 2)
    offset = (targets[:, 0] - position) % ctx_count
    slot = targets[:, 1].reshape(requests, lists)
    peers = jnp.arange(ctx_count, dtype=jnp.int32)
    outgoing = targets[:, 0][None, :] == peers[:, None]
    send_kv = jnp.einsum(
        "pm,mjkc->pjkc", outgoing.astype(jnp.bfloat16), items_kv, preferred_element_type=jnp.float32
    ).astype(jnp.bfloat16)
    send_score = jnp.einsum(
        "pm,mkj->pkj", outgoing.astype(jnp.float32), items_score, precision=HIGHEST
    )
    send_count = jnp.sum(jnp.where(outgoing, items_count[None, :], 0), axis=1)
    recv_kv, recv_score, recv_count = (
        lax.all_to_all(send_kv, "ctx", split_axis=0, concat_axis=0, tiled=True),
        lax.all_to_all(
            send_score.astype(jnp.bfloat16), "ctx", split_axis=0, concat_axis=0, tiled=True
        ).astype(send_score.dtype),
        lax.all_to_all(send_count, "ctx", split_axis=0, concat_axis=0, tiled=True),
    )
    source = (position - offset) % ctx_count
    incoming = source[:, None] == peers[None, :]
    got_kv = jnp.einsum(
        "mp,pjkc->mjkc", incoming.astype(jnp.bfloat16), recv_kv, preferred_element_type=jnp.float32
    ).astype(jnp.bfloat16)
    got_score = jnp.einsum(
        "mp,pkj->mkj", incoming.astype(jnp.float32), recv_score, precision=HIGHEST
    )
    got_count = jnp.sum(jnp.where(incoming, recv_count[None, :], 0), axis=1)
    slot_table = slot[:, None, :] == jnp.arange(lists, dtype=jnp.int32)[None, :, None]
    placed_kv = jnp.einsum(
        "rsb,rbjkc->rsjkc",
        slot_table.astype(jnp.bfloat16),
        got_kv.reshape(requests, lists, width, local_kv, pair),
        preferred_element_type=jnp.float32,
    ).astype(jnp.bfloat16)
    packed_cache = placed_kv.reshape(requests, lists * width, local_kv, pair)
    placed_score = jnp.einsum(
        "rsb,rbkj->rksj",
        slot_table.astype(jnp.float32),
        got_score.reshape(requests, lists, local_kv, width),
        precision=HIGHEST,
    )
    packed_scores = placed_score.reshape(requests, local_kv, lists * width)
    placed_count = jnp.sum(jnp.where(slot_table, got_count.reshape(requests, 1, lists), 0), axis=2)
    live = (jnp.arange(width, dtype=jnp.int32)[None, None, :] < placed_count[:, :, None]).reshape(
        requests, lists * width
    )
    steps = new_tokens.shape[0]
    local_width = new_tokens.shape[2]
    flat = new_tokens.reshape(steps * requests, local_width)
    wide = flat.astype(jnp.float32)
    squares = jnp.sum(wide * wide, axis=1)
    query_part = jnp.dot(flat, w_query, preferred_element_type=jnp.float32)
    pair_part = jnp.dot(
        flat, w_keyval.reshape(local_width, local_kv * pair), preferred_element_type=jnp.float32
    )
    squares, query_part, pair_part = lax.psum((squares, query_part, pair_part), "ctx")
    inverse = lax.rsqrt(squares / D + EPSILON)
    query = (
        (query_part * inverse[:, None])
        .astype(jnp.bfloat16)
        .reshape(steps, requests, local_kv, group, head_size)
    )
    fresh = (
        (pair_part * inverse[:, None]).astype(jnp.bfloat16).reshape(steps, requests, local_kv, pair)
    )
    query = jnp.transpose(query, (1, 2, 0, 3, 4)).reshape(
        requests, local_kv, steps * group, head_size
    )
    fresh = jnp.transpose(fresh, (1, 2, 0, 3))
    logits = (
        jnp.einsum(
            "rkqd,rnkd->rkqn",
            query,
            packed_cache[..., :head_size],
            preferred_element_type=jnp.float32,
        )
        / root_size
    )
    logits = jnp.where(live[:, None, None, :], logits, -jnp.inf)
    top = jnp.max(logits, axis=3)
    weights = jnp.exp(logits - top[..., None])
    totals = jnp.sum(weights, axis=3)
    weighted = jnp.einsum(
        "rkqn,rnkd->rkqd",
        weights.astype(jnp.bfloat16),
        packed_cache[..., head_size:],
        preferred_element_type=jnp.float32,
    )
    top, totals, weighted = joined((top, totals, weighted), "ctx", combine_parts)
    recent = (
        jnp.einsum(
            "rkqd,rkud->rkqu", query, fresh[..., :head_size], preferred_element_type=jnp.float32
        )
        / root_size
    )
    causal = (jnp.arange(steps * group, dtype=jnp.int32) // group)[:, None] >= jnp.arange(
        steps, dtype=jnp.int32
    )[None, :]
    recent = jnp.where(causal[None, None], recent, -jnp.inf)
    best = jnp.maximum(top, jnp.max(recent, axis=3))
    weight_new = jnp.exp(recent - best[..., None])
    factor_old = jnp.exp(top - best)
    normalizer = totals * factor_old + jnp.sum(weight_new, axis=3)
    weighted = weighted * factor_old[..., None] + jnp.einsum(
        "rkqu,rkud->rkqd",
        weight_new.astype(jnp.bfloat16),
        fresh[..., head_size:],
        preferred_element_type=jnp.float32,
    )
    attended = (weighted / normalizer[..., None]).astype(jnp.bfloat16)
    attended = attended.reshape(requests, local_kv, steps, group, head_size)
    attended = jnp.transpose(attended, (2, 0, 1, 3, 4)).reshape(
        steps * requests, local_kv * group * head_size
    )
    partial_value = jnp.dot(attended, w_out, preferred_element_type=jnp.float32)
    summed_out = lax.psum(partial_value, "head")
    decoded = summed_out.astype(jnp.bfloat16).reshape(steps, requests, local_width)
    return (packed_cache, packed_scores, decoded)


def solution(mesh):
    in_specs = (
        P(None, "ctx", "head", None),
        P(None, "ctx", None),
        P(None, "ctx", None),
        P(None, "ctx", "head"),
        P(None, None, "ctx"),
        P("ctx", "head"),
        P("ctx", "head", None),
        P("head", "ctx"),
    )
    out_specs = (P(None, "ctx", "head", None), P(None, "head", "ctx"), P(None, None, "ctx"))
    body = sixteen if mesh.shape["ctx"] == 16 and mesh.shape["head"] == 2 else per_device
    return jax.shard_map(
        body, mesh=mesh, in_specs=in_specs, out_specs=out_specs, check_vma=False
    )
```

```python
import math

import jax
import jax.numpy as jnp
from jax import lax
from jax.experimental import pallas as pl
from jax.experimental.pallas import tpu as pltpu
from jax.sharding import PartitionSpec as P

D = 8192
H = 64
QS = 256
EPSILON = 1e-05
HIGHEST = lax.Precision.HIGHEST
BF = jnp.bfloat16
F32 = jnp.float32
STAT = 144
LARGE = 1e30
VMEM_LIMIT = 48 << 20
ANY = pl.BlockSpec(memory_space=pltpu.HBM)
SMEM = pl.BlockSpec(memory_space=pltpu.SMEM)
VMEM = pl.BlockSpec(memory_space=pltpu.VMEM)
NT = (((1,), (1,)), ((), ()))
TN = (((0,), (0,)), ((), ()))


def hbm(value):
    return pltpu.with_memory_space_constraint(value, pltpu.HBM)


def params():
    return pltpu.CompilerParams(vmem_limit_bytes=VMEM_LIMIT)


def pack_kernel(keep, target, kv, send, spans, blocks, in_sem, out_sem):
    items, width = keep.shape
    span = 2 * width
    lists = items // kv.shape[0]

    def fetch(m):
        return pltpu.make_async_copy(
            kv.at[m // lists, pl.ds((m % lists) * span, span)], spans.at[m, pl.ds(0, span)], in_sem.at[m]
        )

    def put(m):
        return pltpu.make_async_copy(blocks.at[m], send.at[target[m, 0]], out_sem.at[m])

    for m in range(items):
        fetch(m).start()
        spans[m, span] = jnp.zeros(spans.shape[2:], spans.dtype)

    def one(m, carry):
        fetch(m).wait()

        def rows(j, inner):
            values = [spans[m, keep[m, j * 16 + u]] for u in range(16)]
            for u in range(16):
                blocks[m, j * 16 + u] = values[u]
            return inner

        lax.fori_loop(0, width // 16, rows, 0)
        put(m).start()
        return carry

    lax.fori_loop(0, items, one, 0)
    for m in range(items):
        put(m).wait()


def pack(kv_cache, keep, target):
    items, width = keep.shape
    tail = kv_cache.shape[2:]
    return pl.pallas_call(
        pack_kernel,
        out_shape=pltpu.HBM((items, width, *tail), kv_cache.dtype),
        in_specs=[SMEM, SMEM, ANY],
        out_specs=ANY,
        scratch_shapes=[
            pltpu.VMEM((items, 2 * width + 8, *tail), kv_cache.dtype),
            pltpu.VMEM((items, width, *tail), kv_cache.dtype),
            pltpu.SemaphoreType.DMA((items,)),
            pltpu.SemaphoreType.DMA((items,)),
        ],
        compiler_params=params(),
        name="pack_rows",
    )(keep, target, kv_cache)


def terms(value):
    high = value.astype(BF).astype(F32)
    middle = (value - high).astype(BF).astype(F32)
    return high, middle, value - high - middle


def project_kernel(tokens, wq, wkv, samples, out, rows, extra):
    i = pl.program_id(0)
    x = jnp.concatenate([tokens[t, r : r + 1, :].astype(F32) for r in range(2) for t in range(4)], axis=0)
    x = x.astype(BF)
    part = jnp.dot(x, wq[...], preferred_element_type=F32)
    for r in range(2):
        for g in range(8):
            rows[r * 8 + i * 2 + g // 4, (g % 4) * 4 : (g % 4) * 4 + 4, :] = part[
                r * 4 : r * 4 + 4, g * 128 : g * 128 + 128
            ]

    @pl.when(i == 0)
    def _():
        for r in range(2):
            for c in range(32):
                out[r * 8 + c // 4, (c % 4) * 16 : (c % 4) * 16 + 16, :] = samples[
                    r, :, c * 128 : c * 128 + 128
                ]
        heads = pltpu.einshape("nhd->hnd", wkv[...])
        wide = x.astype(F32)
        squares = jnp.sum(wide * wide, axis=1, keepdims=True)
        row = lax.broadcasted_iota(jnp.int32, (8, 128), 0)
        lane = lax.broadcasted_iota(jnp.int32, (8, 128), 1)
        line = jnp.sum(jnp.where(row == lane, squares, 0.0), axis=0, keepdims=True)
        line = jnp.concatenate([line, jnp.zeros((3, 128), F32)], axis=0)
        for p in range(16):
            extra[p, 4:8, :] = line
        for j in range(4):
            pair = jnp.dot(x, heads[j], preferred_element_type=F32)
            for r in range(2):
                for half in range(2):
                    extra[r * 8 + j * 2 + half, 0:4, :] = pair[
                        r * 4 : r * 4 + 4, half * 128 : half * 128 + 128
                    ]

    @pl.when(i == 3)
    def _():
        for at, term in enumerate(terms(rows[...])):
            out[:, 64 + at * 16 : 80 + at * 16, :] = term.astype(BF)
        first, second, third = terms(extra[...])
        out[:, 112:128, :] = jnp.concatenate([first, second], axis=1).astype(BF)
        out[:, 128:144, :] = jnp.concatenate([third, jnp.zeros((16, 8, 128), F32)], axis=1).astype(BF)


def project(tokens, w_query, w_keyval, samples):
    depth, columns = w_query.shape
    step = columns // 4
    return pl.pallas_call(
        project_kernel,
        out_shape=jax.ShapeDtypeStruct((16, 144, 128), BF),
        grid=(4,),
        in_specs=[
            pl.BlockSpec(tokens.shape, lambda i: (0, 0, 0)),
            pl.BlockSpec((depth, step), lambda i: (0, i)),
            pl.BlockSpec(w_keyval.shape, lambda i: (0, 0, 0)),
            pl.BlockSpec(samples.shape, lambda i: (0, 0, 0)),
        ],
        out_specs=pl.BlockSpec((16, 144, 128), lambda i: (0, 0, 0)),
        scratch_shapes=[pltpu.VMEM((16, 16, 128), F32), pltpu.VMEM((16, 8, 128), F32)],
        compiler_params=params(),
        name="project_tokens",
    )(tokens, hbm(w_query), hbm(w_keyval), hbm(samples))


def settle_kernel(place, parts, out):
    request = place[0] // 8
    total = jnp.sum(parts[:, 64:80, :].astype(F32), axis=0)
    total = total + jnp.sum(parts[:, 80:96, :].astype(F32), axis=0)
    total = total + jnp.sum(parts[:, 96:112, :].astype(F32), axis=0)
    both = jnp.sum(parts[:, 112:128, :].astype(F32), axis=0)
    rest = jnp.sum(parts[:, 128:144, :].astype(F32), axis=0)
    both = both[0:8] + both[8:16] + rest[0:8]
    row = lax.broadcasted_iota(jnp.int32, (16, 128), 0)
    lane = lax.broadcasted_iota(jnp.int32, (16, 128), 1)
    squares = jnp.where(lane == request * 4 + row % 4, both[4:5, :], 0.0)
    inverse = lax.rsqrt(jnp.sum(squares, axis=1, keepdims=True) / D + EPSILON)
    own = total * inverse
    fresh = jnp.where(row[0:8] < 4, both * inverse[0:8], 0.0)
    rounded = jnp.concatenate([own, fresh, jnp.zeros((8, 128), F32)], axis=0).astype(BF)
    out[...] = jnp.broadcast_to(rounded[None], out.shape)


def moments_kernel(parts, stat):
    for i in range(4):
        q = parts[:, i * 16 : i * 16 + 16, :].reshape(256, 128)
        second = lax.dot_general(q, q, TN, preferred_element_type=F32)
        mean = jnp.sum(q.astype(F32), axis=0, keepdims=True) / QS
        first = jnp.concatenate([mean, jnp.zeros((7, 128), F32)], axis=0)
        outer = lax.dot_general(first, first, TN, preferred_element_type=F32, precision=HIGHEST)
        cov = second / QS - outer
        scaled = mean / math.sqrt(128)
        high = scaled.astype(BF).astype(F32)
        lines = jnp.concatenate([high, scaled - high, jnp.zeros((14, 128), F32)], axis=0)
        stat[0, i, 0:128, :] = cov.astype(BF)
        stat[0, i, 128:144, :] = lines.astype(BF)


def settle(place, parts):
    return pl.pallas_call(
        settle_kernel,
        out_shape=jax.ShapeDtypeStruct((16, 32, 128), BF),
        in_specs=[SMEM, VMEM],
        out_specs=VMEM,
        compiler_params=params(),
        name="settle_tokens",
    )(place, parts)


def head_moments(parts):
    return pl.pallas_call(
        moments_kernel,
        out_shape=jax.ShapeDtypeStruct((1, 4, STAT, 128), BF),
        in_specs=[VMEM],
        out_specs=VMEM,
        compiler_params=params(),
        name="head_moments",
    )(parts)


def attend_kernel(target, query, bias, send, out, rows, logits, sem):
    items = rows.shape[0]
    width = rows.shape[1]
    wide = width * 4

    def fetch(m):
        return pltpu.make_async_copy(send.at[target[m, 0]], rows.at[m], sem.at[m])

    for m in range(items):
        fetch(m).start()
    head = lax.broadcasted_iota(jnp.int32, (128, wide), 0) // 32
    lane = lax.broadcasted_iota(jnp.int32, (128, wide), 1) % 4
    own = head == lane
    for r in range(2):
        q = query[r * 8 : r * 8 + 8, 0:16, :].reshape(128, 128)
        for b in range(8):
            m = r * 8 + b
            fetch(m).wait()
            keys = rows[m, :, :, 0:128].reshape(wide, 128)
            scores = lax.dot_general(q, keys, NT, preferred_element_type=F32) / math.sqrt(128)
            scores = jnp.where(own, scores, -LARGE) + bias[m : m + 1, :]
            logits[:, b * wide : b * wide + wide] = scores
        top = jnp.max(logits[...], axis=1, keepdims=True)
        total = jnp.zeros((128, 1), F32)
        weighted = jnp.zeros((128, 128), F32)
        for b in range(8):
            weights = jnp.exp(logits[:, b * wide : b * wide + wide] - top)
            total = total + jnp.sum(weights, axis=1, keepdims=True)
            values = rows[r * 8 + b, :, :, 128:256].reshape(wide, 128)
            weighted = weighted + jnp.dot(weights.astype(BF), values, preferred_element_type=F32)
        top_line = jnp.broadcast_to(top, (128, 128)).T[0:1, :]
        total_line = jnp.broadcast_to(total, (128, 128)).T[0:1, :]
        lines = jnp.concatenate([top_line, total_line, jnp.zeros((6, 128), F32)], axis=0)
        for i in range(8):
            out[r * 8 + i, 0:16, :] = weighted[i * 16 : i * 16 + 16, :]
            out[r * 8 + i, 16:24, :] = lines


def attend(target, query, bias, send):
    items, width = send.shape[:2]
    return pl.pallas_call(
        attend_kernel,
        out_shape=jax.ShapeDtypeStruct((16, 24, 128), F32),
        in_specs=[SMEM, VMEM, VMEM, ANY],
        out_specs=VMEM,
        scratch_shapes=[
            pltpu.VMEM(send.shape, send.dtype),
            pltpu.VMEM((128, 8 * width * 4), F32),
            pltpu.SemaphoreType.DMA((items,)),
        ],
        compiler_params=params(),
        name="attend_kept",
    )(target, query, bias, hbm(send))


def combine_kernel(place, target, parts, query, out, scores):
    p = place[0]
    mine = query[p, 0:16, :]
    pair = (p // 2) * 2
    fresh_key = query[pair, 16:32, :]
    fresh_value = query[pair + 1, 16:32, :]
    recent = lax.dot_general(mine, fresh_key, NT, preferred_element_type=F32) / math.sqrt(128)
    step = lax.broadcasted_iota(jnp.int32, (16, 16), 0) % 4
    column = lax.broadcasted_iota(jnp.int32, (16, 16), 1)
    recent = jnp.where(column <= step, recent, -LARGE)
    row = lax.broadcasted_iota(jnp.int32, (16, 128), 0)
    lane = lax.broadcasted_iota(jnp.int32, (16, 128), 1)
    chosen = lane == (p % 8) * 16 + row
    tops, totals = [], []
    for s in range(16):
        tops.append(jnp.sum(jnp.where(chosen, parts[s, 16:17, :], 0.0), axis=1, keepdims=True))
        totals.append(jnp.sum(jnp.where(chosen, parts[s, 17:18, :], 0.0), axis=1, keepdims=True))
    best = jnp.max(recent, axis=1, keepdims=True)
    for s in range(16):
        best = jnp.maximum(best, tops[s])
    weights = jnp.exp(recent - best)
    total = jnp.sum(weights, axis=1, keepdims=True)
    weighted = jnp.dot(weights.astype(BF), fresh_value, preferred_element_type=F32)
    for s in range(16):
        factor = jnp.exp(tops[s] - best)
        total = total + totals[s] * factor
        weighted = weighted + parts[s, 0:16, :] * factor
    out[...] = jnp.broadcast_to((weighted / total).astype(BF)[None], out.shape)
    for m in range(16):
        start = pl.multiple_of(target[m, 1] * 128, 128)
        scores[m // 8, :, pl.ds(start, 128)] = parts[sender(m, p, target, 16), 18:22, :]


def combine(place, target, parts, query):
    return pl.pallas_call(
        combine_kernel,
        out_shape=(
            jax.ShapeDtypeStruct((16, 16, 128), BF),
            jax.ShapeDtypeStruct((2, 4, 1024), F32),
        ),
        in_specs=[SMEM, SMEM, VMEM, VMEM],
        out_specs=(VMEM, VMEM),
        compiler_params=params(),
        name="combine_parts",
    )(place, target, parts, query)


def reverse_bits(value, order):
    place = 0
    for at, bit in enumerate(order):
        place = place + ((value // bit) % 2) * (1 << at)
    return place


def score_kernel(orders, place, target, stat_a, stat_b, send, parts, out, blocks, sem):
    items = blocks.shape[0]
    lists = items // 2
    me = place[0]

    def fetch(m):
        return pltpu.make_async_copy(send.at[target[m, 0]], blocks.at[m], sem.at[m])

    for m in range(items):
        fetch(m).start()
    out[...] = parts[...]
    for m in range(items):
        fetch(m).wait()
    for r in range(2):
        for j in range(4):
            tables = []
            for o in range(2):
                owner = jnp.bitwise_xor(me, r * 8 + j * 2 + o)
                for half, stat in enumerate((stat_a, stat_b)):
                    tables.append(stat[reverse_bits(owner, orders[half])].reshape(2 * STAT, 128))
            for c in range(lists // 2):
                first = r * lists + c * 2
                keys = blocks[first : first + 2, :, j, 0:128].reshape(256, 128)
                flipped = keys.astype(F32).T
                logits = []
                for table in tables:
                    turned = lax.dot_general(table, keys, NT, preferred_element_type=F32)
                    for g in range(2):
                        base = g * STAT
                        quadratic = jnp.sum(
                            turned[base : base + 128] * flipped, axis=0, keepdims=True
                        )
                        linear = turned[base + 128 : base + 129] + turned[base + 129 : base + 130]
                        logits.append(linear + quadratic / 256.0)
                logit = jnp.concatenate(logits, axis=0)
                top = jnp.max(logit, axis=0, keepdims=True)
                mean = jnp.sum(jnp.exp(logit - top), axis=0, keepdims=True) / 8.0
                line = top + jnp.log(mean)
                for u in range(2):
                    p = target[first + u, 0]
                    out[p, 18 + j : 19 + j, :] = line[:, u * 128 : u * 128 + 128]


def score(orders, place, target, stat_a, stat_b, send, parts):
    items = send.shape[0]

    def kernel(*refs):
        score_kernel(orders, *refs)

    return pl.pallas_call(
        kernel,
        out_shape=jax.ShapeDtypeStruct(parts.shape, parts.dtype),
        in_specs=[SMEM, SMEM, VMEM, VMEM, ANY, VMEM],
        out_specs=VMEM,
        scratch_shapes=[
            pltpu.VMEM(send.shape, send.dtype),
            pltpu.SemaphoreType.DMA((items,)),
        ],
        compiler_params=params(),
        name="score_kept",
    )(place, target, stat_a, stat_b, hbm(send), parts)


def sender(m, me, target, count):
    return (2 * me - target[m, 0] + count) % count


def place_kernel(place, target, arrived, packed, blocks, in_sem, out_sem):
    items = arrived.shape[0]
    lists = items // 2

    def fetch(m):
        return pltpu.make_async_copy(
            arrived.at[sender(m, place[0], target, items)], blocks.at[m], in_sem.at[m]
        )

    def put(m):
        slot = (m // lists) * lists + target[m, 1]
        return pltpu.make_async_copy(blocks.at[m], packed.at[slot], out_sem.at[m])

    for m in range(items):
        fetch(m).start()
    for m in range(items):
        fetch(m).wait()
        put(m).start()
    for m in range(items):
        put(m).wait()


def put_blocks(place, target, arrived):
    items = arrived.shape[0]
    return pl.pallas_call(
        place_kernel,
        out_shape=pltpu.HBM(arrived.shape, arrived.dtype),
        in_specs=[SMEM, SMEM, ANY],
        out_specs=ANY,
        scratch_shapes=[
            pltpu.VMEM(arrived.shape, arrived.dtype),
            pltpu.SemaphoreType.DMA((items,)),
            pltpu.SemaphoreType.DMA((items,)),
        ],
        compiler_params=params(),
        name="place_blocks",
    )(place, target, hbm(arrived))


def exchange(value):
    return lax.all_to_all(value, "ctx", split_axis=0, concat_axis=0, tiled=True)


def doubled(value, bit):
    pairs = [(i, i ^ bit) for i in range(16)]
    return jnp.concatenate([value, lax.ppermute(value, "ctx", pairs)], axis=0)


def after(values, token):
    return lax.optimization_barrier((values, token))[0]


ORDERS = ((8, 4, 2, 1), (8, 4, 1, 2))


def sixteen(
    kv_cache, keep_rows, block_target, future_queries, new_tokens, w_query, w_keyval, w_out
):
    requests, cache_rows, local_kv, pair = kv_cache.shape
    lists, width = keep_rows.shape[1:]
    items = requests * lists
    keep = keep_rows.reshape(items, width)
    target = block_target.reshape(items, 2)
    place = lax.axis_index("ctx").astype(jnp.int32).reshape(1)
    parts = exchange(project(new_tokens, w_query, w_keyval, future_queries))
    send = pack(kv_cache, keep, target)
    parts = after(parts, send)
    own = settle(place, parts)
    query = exchange(own)
    stat = head_moments(after(parts, own))
    stat = doubled(doubled(stat, 8), 4)
    arrived = exchange(after(send, (query, stat)))
    bias = jnp.where(after(keep, query) < 2 * width, 0.0, -LARGE).astype(F32)
    bias = jnp.broadcast_to(bias[:, :, None], (items, width, 4)).reshape(items, width * 4)
    stat_a = doubled(doubled(stat[:, :2], 2), 1)
    stat_b = doubled(doubled(stat[:, 2:], 1), 2)
    softmax = attend(target, query, bias, send)
    softmax = score(ORDERS, place, target, stat_a, stat_b, send, softmax)
    parts = exchange(after(softmax, arrived))
    packed = put_blocks(place, target, arrived)
    share, scores = combine(place, target, after(parts, packed), query)
    attended = exchange(share)
    rows = attended.reshape(requests, 32, 4, 128)
    rows = jnp.transpose(rows, (2, 0, 1, 3)).reshape(8, 4096)
    partial_value = jnp.dot(rows, w_out, preferred_element_type=F32)
    decoded = lax.psum(partial_value, "head").astype(BF).reshape(4, requests, w_out.shape[1])
    return packed.reshape(requests, lists * width, local_kv, pair), scores, decoded


def joined(value, axis, join):
    pieces = jax.tree.map(lambda part: lax.all_gather(part, axis), value)
    head = jax.tree.map(lambda part: part[0], pieces)
    tail = jax.tree.map(lambda part: part[1:], pieces)
    running, _ = lax.scan(lambda running, share: (join(running, share), None), head, tail)
    return running


def group_scores(keys, mean_q, cov_q):
    lifted = keys.astype(jnp.float32)
    linear = jnp.einsum("nkd,kgd->nkg", lifted, mean_q, precision=HIGHEST)
    turned = jnp.einsum("nkd,kgde->nkge", lifted, cov_q, precision=HIGHEST)
    quadratic = jnp.sum(turned * lifted[:, :, None, :], axis=-1)
    logits = linear / math.sqrt(keys.shape[-1]) + quadratic / (2.0 * keys.shape[-1])
    top = jnp.max(logits, axis=2)
    return top + jnp.log(jnp.mean(jnp.exp(logits - top[:, :, None]), axis=2))


def combine_parts(first, second):
    top_a, total_a, weighted_a = first
    top_b, total_b, weighted_b = second
    best = jnp.maximum(top_a, top_b)
    factor_a = jnp.exp(top_a - best)
    factor_b = jnp.exp(top_b - best)
    return (
        best,
        total_a * factor_a + total_b * factor_b,
        weighted_a * factor_a[..., None] + weighted_b * factor_b[..., None],
    )


def moments(sample):
    second = jnp.einsum("rshd,rshe->rhde", sample, sample, preferred_element_type=jnp.float32)
    summed = jnp.sum(sample.astype(jnp.float32), axis=1)
    return (second, summed)


KVH = 8


def per_device(
    kv_cache, keep_rows, block_target, future_queries, new_tokens, w_query, w_keyval, w_out
):
    requests, cache_rows, local_kv, pair = kv_cache.shape
    head_size = pair // 2
    lists, width = (keep_rows.shape[1], keep_rows.shape[2])
    span = 2 * width
    group = H // KVH
    ctx_count = lax.axis_size("ctx")
    position = lax.axis_index("ctx")
    root_size = math.sqrt(head_size)
    sample = future_queries.reshape(requests, -1, local_kv * group, head_size)
    second, summed = moments(sample)
    second, summed = lax.psum((second, summed), "ctx")
    mean_q = summed / QS
    cov_q = second / QS - mean_q[..., :, None] * mean_q[..., None, :]
    mean_q = mean_q.reshape(requests, local_kv, group, head_size)
    cov_q = cov_q.reshape(requests, local_kv, group, head_size, head_size)
    span_index = jnp.arange(span, dtype=jnp.int32)
    block_kv, block_score, block_count = ([], [], [])
    for request in range(requests):
        listed = keep_rows[request]
        picker = (listed[:, :, None] == span_index[None, None, :]).astype(jnp.bfloat16)
        spans = kv_cache[request].reshape(lists, span, local_kv * pair)
        chosen = jnp.einsum(
            "bjs,bsc->bjc", picker, spans, preferred_element_type=jnp.float32
        ).astype(jnp.bfloat16)
        chosen = chosen.reshape(lists, width, local_kv, pair)
        every = group_scores(kv_cache[request][:, :, :head_size], mean_q[request], cov_q[request])
        every = every.reshape(lists, span, local_kv)
        picked = jnp.einsum("bjs,bsk->bkj", picker.astype(jnp.float32), every, precision=HIGHEST)
        block_kv.append(chosen)
        block_score.append(picked)
        block_count.append(jnp.sum((listed < span).astype(jnp.int32), axis=1))
    items_kv = jnp.concatenate(block_kv, axis=0)
    items_score = jnp.concatenate(block_score, axis=0)
    items_count = jnp.concatenate(block_count, axis=0)
    total_items = requests * lists
    targets = block_target.reshape(total_items, 2)
    offset = (targets[:, 0] - position) % ctx_count
    slot = targets[:, 1].reshape(requests, lists)
    peers = jnp.arange(ctx_count, dtype=jnp.int32)
    outgoing = targets[:, 0][None, :] == peers[:, None]
    send_kv = jnp.einsum(
        "pm,mjkc->pjkc", outgoing.astype(jnp.bfloat16), items_kv, preferred_element_type=jnp.float32
    ).astype(jnp.bfloat16)
    send_score = jnp.einsum(
        "pm,mkj->pkj", outgoing.astype(jnp.float32), items_score, precision=HIGHEST
    )
    send_count = jnp.sum(jnp.where(outgoing, items_count[None, :], 0), axis=1)
    recv_kv, recv_score, recv_count = (
        lax.all_to_all(send_kv, "ctx", split_axis=0, concat_axis=0, tiled=True),
        lax.all_to_all(
            send_score.astype(jnp.bfloat16), "ctx", split_axis=0, concat_axis=0, tiled=True
        ).astype(send_score.dtype),
        lax.all_to_all(send_count, "ctx", split_axis=0, concat_axis=0, tiled=True),
    )
    source = (position - offset) % ctx_count
    incoming = source[:, None] == peers[None, :]
    got_kv = jnp.einsum(
        "mp,pjkc->mjkc", incoming.astype(jnp.bfloat16), recv_kv, preferred_element_type=jnp.float32
    ).astype(jnp.bfloat16)
    got_score = jnp.einsum(
        "mp,pkj->mkj", incoming.astype(jnp.float32), recv_score, precision=HIGHEST
    )
    got_count = jnp.sum(jnp.where(incoming, recv_count[None, :], 0), axis=1)
    slot_table = slot[:, None, :] == jnp.arange(lists, dtype=jnp.int32)[None, :, None]
    placed_kv = jnp.einsum(
        "rsb,rbjkc->rsjkc",
        slot_table.astype(jnp.bfloat16),
        got_kv.reshape(requests, lists, width, local_kv, pair),
        preferred_element_type=jnp.float32,
    ).astype(jnp.bfloat16)
    packed_cache = placed_kv.reshape(requests, lists * width, local_kv, pair)
    placed_score = jnp.einsum(
        "rsb,rbkj->rksj",
        slot_table.astype(jnp.float32),
        got_score.reshape(requests, lists, local_kv, width),
        precision=HIGHEST,
    )
    packed_scores = placed_score.reshape(requests, local_kv, lists * width)
    placed_count = jnp.sum(jnp.where(slot_table, got_count.reshape(requests, 1, lists), 0), axis=2)
    live = (jnp.arange(width, dtype=jnp.int32)[None, None, :] < placed_count[:, :, None]).reshape(
        requests, lists * width
    )
    steps = new_tokens.shape[0]
    local_width = new_tokens.shape[2]
    flat = new_tokens.reshape(steps * requests, local_width)
    wide = flat.astype(jnp.float32)
    squares = jnp.sum(wide * wide, axis=1)
    query_part = jnp.dot(flat, w_query, preferred_element_type=jnp.float32)
    pair_part = jnp.dot(
        flat, w_keyval.reshape(local_width, local_kv * pair), preferred_element_type=jnp.float32
    )
    squares, query_part, pair_part = lax.psum((squares, query_part, pair_part), "ctx")
    inverse = lax.rsqrt(squares / D + EPSILON)
    query = (
        (query_part * inverse[:, None])
        .astype(jnp.bfloat16)
        .reshape(steps, requests, local_kv, group, head_size)
    )
    fresh = (
        (pair_part * inverse[:, None]).astype(jnp.bfloat16).reshape(steps, requests, local_kv, pair)
    )
    query = jnp.transpose(query, (1, 2, 0, 3, 4)).reshape(
        requests, local_kv, steps * group, head_size
    )
    fresh = jnp.transpose(fresh, (1, 2, 0, 3))
    logits = (
        jnp.einsum(
            "rkqd,rnkd->rkqn",
            query,
            packed_cache[..., :head_size],
            preferred_element_type=jnp.float32,
        )
        / root_size
    )
    logits = jnp.where(live[:, None, None, :], logits, -jnp.inf)
    top = jnp.max(logits, axis=3)
    weights = jnp.exp(logits - top[..., None])
    totals = jnp.sum(weights, axis=3)
    weighted = jnp.einsum(
        "rkqn,rnkd->rkqd",
        weights.astype(jnp.bfloat16),
        packed_cache[..., head_size:],
        preferred_element_type=jnp.float32,
    )
    top, totals, weighted = joined((top, totals, weighted), "ctx", combine_parts)
    recent = (
        jnp.einsum(
            "rkqd,rkud->rkqu", query, fresh[..., :head_size], preferred_element_type=jnp.float32
        )
        / root_size
    )
    causal = (jnp.arange(steps * group, dtype=jnp.int32) // group)[:, None] >= jnp.arange(
        steps, dtype=jnp.int32
    )[None, :]
    recent = jnp.where(causal[None, None], recent, -jnp.inf)
    best = jnp.maximum(top, jnp.max(recent, axis=3))
    weight_new = jnp.exp(recent - best[..., None])
    factor_old = jnp.exp(top - best)
    normalizer = totals * factor_old + jnp.sum(weight_new, axis=3)
    weighted = weighted * factor_old[..., None] + jnp.einsum(
        "rkqu,rkud->rkqd",
        weight_new.astype(jnp.bfloat16),
        fresh[..., head_size:],
        preferred_element_type=jnp.float32,
    )
    attended = (weighted / normalizer[..., None]).astype(jnp.bfloat16)
    attended = attended.reshape(requests, local_kv, steps, group, head_size)
    attended = jnp.transpose(attended, (2, 0, 1, 3, 4)).reshape(
        steps * requests, local_kv * group * head_size
    )
    partial_value = jnp.dot(attended, w_out, preferred_element_type=jnp.float32)
    summed_out = lax.psum(partial_value, "head")
    decoded = summed_out.astype(jnp.bfloat16).reshape(steps, requests, local_width)
    return (packed_cache, packed_scores, decoded)


def solution(mesh):
    in_specs = (
        P(None, "ctx", "head", None),
        P(None, "ctx", None),
        P(None, "ctx", None),
        P(None, "ctx", "head"),
        P(None, None, "ctx"),
        P("ctx", "head"),
        P("ctx", "head", None),
        P("head", "ctx"),
    )
    out_specs = (P(None, "ctx", "head", None), P(None, "head", "ctx"), P(None, None, "ctx"))
    body = sixteen if mesh.shape["ctx"] == 16 and mesh.shape["head"] == 2 else per_device
    return jax.shard_map(
        body, mesh=mesh, in_specs=in_specs, out_specs=out_specs, check_vma=False
    )
```

```python
import math

import jax
import jax.numpy as jnp
from jax import lax
from jax.experimental import pallas as pl
from jax.experimental.pallas import tpu as pltpu
from jax.sharding import PartitionSpec as P

D = 8192
H = 64
QS = 256
EPSILON = 1e-05
HIGHEST = lax.Precision.HIGHEST
BF = jnp.bfloat16
F32 = jnp.float32
STAT = 144
LARGE = 1e30
ANY = pl.BlockSpec(memory_space=pltpu.HBM)
SMEM = pl.BlockSpec(memory_space=pltpu.SMEM)
VMEM = pl.BlockSpec(memory_space=pltpu.VMEM)
NT = (((1,), (1,)), ((), ()))
TN = (((0,), (0,)), ((), ()))


def hbm(value):
    return pltpu.with_memory_space_constraint(value, pltpu.HBM)


def params(megabytes=8):
    return pltpu.CompilerParams(vmem_limit_bytes=megabytes << 20)


def pack_kernel(keep, target, kv, send, spans, blocks, in_sem, out_sem):
    items, width = keep.shape
    span = 2 * width
    lists = items // kv.shape[0]

    def fetch(m):
        return pltpu.make_async_copy(
            kv.at[m // lists, pl.ds((m % lists) * span, span)], spans.at[m, pl.ds(0, span)], in_sem.at[m]
        )

    def put(m):
        return pltpu.make_async_copy(blocks.at[m], send.at[target[m, 0]], out_sem.at[m])

    for m in range(items):
        fetch(m).start()
        spans[m, span] = jnp.zeros(spans.shape[2:], spans.dtype)

    def one(m, carry):
        fetch(m).wait()

        def rows(j, inner):
            values = [spans[m, keep[m, j * 16 + u]] for u in range(16)]
            for u in range(16):
                blocks[m, j * 16 + u] = values[u]
            return inner

        lax.fori_loop(0, width // 16, rows, 0)
        put(m).start()
        return carry

    lax.fori_loop(0, items, one, 0)
    for m in range(items):
        put(m).wait()


def pack(kv_cache, keep, target):
    items, width = keep.shape
    tail = kv_cache.shape[2:]
    return pl.pallas_call(
        pack_kernel,
        out_shape=pltpu.HBM((items, width, *tail), kv_cache.dtype),
        in_specs=[SMEM, SMEM, ANY],
        out_specs=ANY,
        scratch_shapes=[
            pltpu.VMEM((items, 2 * width + 8, *tail), kv_cache.dtype),
            pltpu.VMEM((items, width, *tail), kv_cache.dtype),
            pltpu.SemaphoreType.DMA((items,)),
            pltpu.SemaphoreType.DMA((items,)),
        ],
        compiler_params=params(20),
        name="pack_rows",
    )(keep, target, hbm(kv_cache))


def split_kernel(samples, out):
    for r in range(2):
        for c in range(32):
            out[r * 8 + c // 4, (c % 4) * 16 : (c % 4) * 16 + 16, :] = samples[
                r, :, c * 128 : c * 128 + 128
            ]


def split_samples(samples):
    return pl.pallas_call(
        split_kernel,
        out_shape=jax.ShapeDtypeStruct((16, 64, 128), BF),
        in_specs=[VMEM],
        out_specs=VMEM,
        compiler_params=params(),
        name="split_samples",
    )(samples)


def project_kernel(tokens, wq, wkv, out):
    i = pl.program_id(0)
    x = jnp.concatenate([tokens[t, r : r + 1, :].astype(F32) for r in range(2) for t in range(4)], axis=0)
    x = x.astype(BF)
    part = jnp.dot(x, wq[...], preferred_element_type=F32)
    for r in range(2):
        for g in range(8):
            out[r * 8 + i * 2 + g // 4, (g % 4) * 4 : (g % 4) * 4 + 4, :] = part[
                r * 4 : r * 4 + 4, g * 128 : g * 128 + 128
            ]

    @pl.when(i == 0)
    def _():
        heads = pltpu.einshape("nhd->hnd", wkv[...])
        wide = x.astype(F32)
        squares = jnp.sum(wide * wide, axis=1, keepdims=True)
        row = lax.broadcasted_iota(jnp.int32, (8, 128), 0)
        lane = lax.broadcasted_iota(jnp.int32, (8, 128), 1)
        line = jnp.sum(jnp.where(row == lane, squares, 0.0), axis=0, keepdims=True)
        line = jnp.concatenate([line, jnp.zeros((3, 128), F32)], axis=0)
        for p in range(16):
            out[p, 20:24, :] = line
        for j in range(4):
            pair = jnp.dot(x, heads[j], preferred_element_type=F32)
            for r in range(2):
                for half in range(2):
                    out[r * 8 + j * 2 + half, 16:20, :] = pair[
                        r * 4 : r * 4 + 4, half * 128 : half * 128 + 128
                    ]


def project(tokens, w_query, w_keyval):
    depth, columns = w_query.shape
    step = columns // 4
    return pl.pallas_call(
        project_kernel,
        out_shape=jax.ShapeDtypeStruct((16, 24, 128), F32),
        grid=(4,),
        in_specs=[
            pl.BlockSpec(tokens.shape, lambda i: (0, 0, 0)),
            pl.BlockSpec((depth, step), lambda i: (0, i)),
            pl.BlockSpec(w_keyval.shape, lambda i: (0, 0, 0)),
        ],
        out_specs=pl.BlockSpec((16, 24, 128), lambda i: (0, 0, 0)),
        compiler_params=params(16),
        name="project_tokens",
    )(hbm(tokens), hbm(w_query), hbm(w_keyval))


def normalize_kernel(place, parts, out):
    total = jnp.sum(parts[...], axis=0)
    request = place[0] // 8
    row = lax.broadcasted_iota(jnp.int32, (24, 128), 0)
    lane = lax.broadcasted_iota(jnp.int32, (24, 128), 1)
    squares = jnp.where(lane == request * 4 + row % 4, total[20:21, :], 0.0)
    inverse = lax.rsqrt(jnp.sum(squares, axis=1, keepdims=True) / D + EPSILON)
    scaled = jnp.where(row < 20, total * inverse, 0.0)
    rounded = jnp.concatenate([scaled, jnp.zeros((8, 128), F32)], axis=0).astype(BF)
    out[...] = jnp.broadcast_to(rounded[None], out.shape)


def normalize(place, parts):
    return pl.pallas_call(
        normalize_kernel,
        out_shape=jax.ShapeDtypeStruct((16, 32, 128), BF),
        in_specs=[SMEM, VMEM],
        out_specs=VMEM,
        compiler_params=params(),
        name="normalize_tokens",
    )(place, parts)


def moments_kernel(parts, stat):
    for i in range(4):
        q = parts[:, i * 16 : i * 16 + 16, :].reshape(256, 128)
        second = lax.dot_general(q, q, TN, preferred_element_type=F32)
        mean = jnp.sum(q.astype(F32), axis=0, keepdims=True) / QS
        first = jnp.concatenate([mean, jnp.zeros((7, 128), F32)], axis=0)
        outer = lax.dot_general(first, first, TN, preferred_element_type=F32, precision=HIGHEST)
        cov = second / QS - outer
        scaled = mean / math.sqrt(128)
        high = scaled.astype(BF).astype(F32)
        lines = jnp.concatenate([high, scaled - high, jnp.zeros((14, 128), F32)], axis=0)
        stat[0, i, 0:128, :] = cov.astype(BF)
        stat[0, i, 128:144, :] = lines.astype(BF)


def head_moments(parts):
    return pl.pallas_call(
        moments_kernel,
        out_shape=jax.ShapeDtypeStruct((1, 4, STAT, 128), BF),
        in_specs=[VMEM],
        out_specs=VMEM,
        compiler_params=params(),
        name="head_moments",
    )(parts)


def attend_kernel(target, query, bias, send, out, rows, logits, sem):
    items = rows.shape[0]
    width = rows.shape[1]
    wide = width * 4

    def fetch(m):
        return pltpu.make_async_copy(send.at[target[m, 0]], rows.at[m], sem.at[m])

    for m in range(items):
        fetch(m).start()
    head = lax.broadcasted_iota(jnp.int32, (128, wide), 0) // 32
    lane = lax.broadcasted_iota(jnp.int32, (128, wide), 1) % 4
    own = head == lane
    for r in range(2):
        q = query[r * 8 : r * 8 + 8, 0:16, :].reshape(128, 128)
        for b in range(8):
            m = r * 8 + b
            fetch(m).wait()
            keys = rows[m, :, :, 0:128].reshape(wide, 128)
            scores = lax.dot_general(q, keys, NT, preferred_element_type=F32) / math.sqrt(128)
            scores = jnp.where(own, scores, -LARGE) + bias[m : m + 1, :]
            logits[:, b * wide : b * wide + wide] = scores
        top = jnp.max(logits[...], axis=1, keepdims=True)
        total = jnp.zeros((128, 1), F32)
        weighted = jnp.zeros((128, 128), F32)
        for b in range(8):
            weights = jnp.exp(logits[:, b * wide : b * wide + wide] - top)
            total = total + jnp.sum(weights, axis=1, keepdims=True)
            values = rows[r * 8 + b, :, :, 128:256].reshape(wide, 128)
            weighted = weighted + jnp.dot(weights.astype(BF), values, preferred_element_type=F32)
        top_line = jnp.broadcast_to(top, (128, 128)).T[0:1, :]
        total_line = jnp.broadcast_to(total, (128, 128)).T[0:1, :]
        lines = jnp.concatenate([top_line, total_line, jnp.zeros((6, 128), F32)], axis=0)
        for i in range(8):
            out[r * 8 + i, 0:16, :] = weighted[i * 16 : i * 16 + 16, :]
            out[r * 8 + i, 16:24, :] = lines


def attend(target, query, bias, send):
    items, width = send.shape[:2]
    return pl.pallas_call(
        attend_kernel,
        out_shape=jax.ShapeDtypeStruct((16, 24, 128), F32),
        in_specs=[SMEM, VMEM, VMEM, ANY],
        out_specs=VMEM,
        scratch_shapes=[
            pltpu.VMEM(send.shape, send.dtype),
            pltpu.VMEM((128, 8 * width * 4), F32),
            pltpu.SemaphoreType.DMA((items,)),
        ],
        compiler_params=params(16),
        name="attend_kept",
    )(target, query, bias, hbm(send))


def combine_kernel(place, target, parts, query, out, scores):
    p = place[0]
    mine = query[p, 0:16, :]
    pair = (p // 2) * 2
    fresh_key = query[pair, 16:32, :]
    fresh_value = query[pair + 1, 16:32, :]
    recent = lax.dot_general(mine, fresh_key, NT, preferred_element_type=F32) / math.sqrt(128)
    step = lax.broadcasted_iota(jnp.int32, (16, 16), 0) % 4
    column = lax.broadcasted_iota(jnp.int32, (16, 16), 1)
    recent = jnp.where(column <= step, recent, -LARGE)
    row = lax.broadcasted_iota(jnp.int32, (16, 128), 0)
    lane = lax.broadcasted_iota(jnp.int32, (16, 128), 1)
    chosen = lane == (p % 8) * 16 + row
    tops, totals = [], []
    for s in range(16):
        tops.append(jnp.sum(jnp.where(chosen, parts[s, 16:17, :], 0.0), axis=1, keepdims=True))
        totals.append(jnp.sum(jnp.where(chosen, parts[s, 17:18, :], 0.0), axis=1, keepdims=True))
    best = jnp.max(recent, axis=1, keepdims=True)
    for s in range(16):
        best = jnp.maximum(best, tops[s])
    weights = jnp.exp(recent - best)
    total = jnp.sum(weights, axis=1, keepdims=True)
    weighted = jnp.dot(weights.astype(BF), fresh_value, preferred_element_type=F32)
    for s in range(16):
        factor = jnp.exp(tops[s] - best)
        total = total + totals[s] * factor
        weighted = weighted + parts[s, 0:16, :] * factor
    out[...] = jnp.broadcast_to((weighted / total).astype(BF)[None], out.shape)
    for m in range(16):
        start = pl.multiple_of(target[m, 1] * 128, 128)
        scores[m // 8, :, pl.ds(start, 128)] = parts[sender(m, p, target, 16), 18:22, :]


def combine(place, target, parts, query):
    return pl.pallas_call(
        combine_kernel,
        out_shape=(
            jax.ShapeDtypeStruct((16, 16, 128), BF),
            jax.ShapeDtypeStruct((2, 4, 1024), F32),
        ),
        in_specs=[SMEM, SMEM, VMEM, VMEM],
        out_specs=(VMEM, VMEM),
        compiler_params=params(),
        name="combine_parts",
    )(place, target, parts, query)


def reverse_bits(value, order):
    place = 0
    for at, bit in enumerate(order):
        place = place + ((value // bit) % 2) * (1 << at)
    return place


def score_kernel(orders, place, target, stat_a, stat_b, send, parts, out, blocks, sem):
    items = blocks.shape[0]
    lists = items // 2
    me = place[0]

    def fetch(m):
        return pltpu.make_async_copy(send.at[target[m, 0]], blocks.at[m], sem.at[m])

    for m in range(items):
        fetch(m).start()
    out[...] = parts[...]
    for m in range(items):
        fetch(m).wait()
    for r in range(2):
        for j in range(4):
            tables = []
            for o in range(2):
                owner = jnp.bitwise_xor(me, r * 8 + j * 2 + o)
                for half, stat in enumerate((stat_a, stat_b)):
                    tables.append(stat[reverse_bits(owner, orders[half])].reshape(2 * STAT, 128))
            for c in range(lists // 2):
                first = r * lists + c * 2
                keys = blocks[first : first + 2, :, j, 0:128].reshape(256, 128)
                flipped = keys.astype(F32).T
                logits = []
                for table in tables:
                    turned = lax.dot_general(table, keys, NT, preferred_element_type=F32)
                    for g in range(2):
                        base = g * STAT
                        quadratic = jnp.sum(
                            turned[base : base + 128] * flipped, axis=0, keepdims=True
                        )
                        linear = turned[base + 128 : base + 129] + turned[base + 129 : base + 130]
                        logits.append(linear + quadratic / 256.0)
                logit = jnp.concatenate(logits, axis=0)
                top = jnp.max(logit, axis=0, keepdims=True)
                mean = jnp.sum(jnp.exp(logit - top), axis=0, keepdims=True) / 8.0
                line = top + jnp.log(mean)
                for u in range(2):
                    p = target[first + u, 0]
                    out[p, 18 + j : 19 + j, :] = line[:, u * 128 : u * 128 + 128]


def score(orders, place, target, stat_a, stat_b, send, parts):
    items = send.shape[0]

    def kernel(*refs):
        score_kernel(orders, *refs)

    return pl.pallas_call(
        kernel,
        out_shape=jax.ShapeDtypeStruct(parts.shape, parts.dtype),
        in_specs=[SMEM, SMEM, VMEM, VMEM, ANY, VMEM],
        out_specs=VMEM,
        scratch_shapes=[
            pltpu.VMEM(send.shape, send.dtype),
            pltpu.SemaphoreType.DMA((items,)),
        ],
        compiler_params=params(24),
        name="score_kept",
    )(place, target, stat_a, stat_b, hbm(send), parts)


def sender(m, me, target, count):
    return (2 * me - target[m, 0] + count) % count


def place_kernel(place, target, arrived, packed, blocks, in_sem, out_sem):
    items = arrived.shape[0]
    lists = items // 2

    def fetch(m):
        return pltpu.make_async_copy(
            arrived.at[sender(m, place[0], target, items)], blocks.at[m], in_sem.at[m]
        )

    def put(m):
        slot = (m // lists) * lists + target[m, 1]
        return pltpu.make_async_copy(blocks.at[m], packed.at[slot], out_sem.at[m])

    for m in range(items):
        fetch(m).start()
    for m in range(items):
        fetch(m).wait()
        put(m).start()
    for m in range(items):
        put(m).wait()


def put_blocks(place, target, arrived):
    items = arrived.shape[0]
    return pl.pallas_call(
        place_kernel,
        out_shape=pltpu.HBM(arrived.shape, arrived.dtype),
        in_specs=[SMEM, SMEM, ANY],
        out_specs=ANY,
        scratch_shapes=[
            pltpu.VMEM(arrived.shape, arrived.dtype),
            pltpu.SemaphoreType.DMA((items,)),
            pltpu.SemaphoreType.DMA((items,)),
        ],
        compiler_params=params(),
        name="place_blocks",
    )(place, target, hbm(arrived))


def finish_kernel(joined, w, out, rows):
    for r in range(2):
        for h in range(32):
            at = (h % 4) * 4
            rows[r * 4 : r * 4 + 4, h * 128 : h * 128 + 128] = joined[
                r * 8 + h // 4, at : at + 4, :
            ].astype(F32)
    value = jnp.dot(rows[...].astype(BF), w[...], preferred_element_type=F32)
    for r in range(2):
        for t in range(4):
            out[t, r : r + 1, :] = value[r * 4 + t : r * 4 + t + 1, :]


def finish(joined, w_out):
    return pl.pallas_call(
        finish_kernel,
        out_shape=jax.ShapeDtypeStruct((4, 2, w_out.shape[1]), F32),
        in_specs=[VMEM, VMEM],
        out_specs=VMEM,
        scratch_shapes=[pltpu.VMEM((8, w_out.shape[0]), F32)],
        compiler_params=params(),
        name="project_out",
    )(joined, w_out)


def exchange(value):
    return lax.all_to_all(value, "ctx", split_axis=0, concat_axis=0, tiled=True)


def doubled(value, bit):
    pairs = [(i, i ^ bit) for i in range(16)]
    return jnp.concatenate([value, lax.ppermute(value, "ctx", pairs)], axis=0)


def after(values, token):
    return lax.optimization_barrier((values, token))[0]


ORDERS = ((8, 4, 2, 1), (8, 4, 1, 2))


def sixteen(
    kv_cache, keep_rows, block_target, future_queries, new_tokens, w_query, w_keyval, w_out
):
    requests, cache_rows, local_kv, pair = kv_cache.shape
    lists, width = keep_rows.shape[1:]
    items = requests * lists
    keep = keep_rows.reshape(items, width)
    target = block_target.reshape(items, 2)
    place = lax.axis_index("ctx").astype(jnp.int32).reshape(1)
    samples = exchange(split_samples(future_queries))
    parts, samples = lax.optimization_barrier((project(new_tokens, w_query, w_keyval), samples))
    parts = exchange(parts)
    stat = doubled(head_moments(samples), 8)
    send = pack(kv_cache, after(keep, samples), target)
    stat = doubled(after(stat, send), 4)
    query = exchange(normalize(place, after(parts, send)))
    arrived = exchange(after(send, (query, stat)))
    bias = jnp.where(after(keep, query) < 2 * width, 0.0, -LARGE).astype(F32)
    bias = jnp.broadcast_to(bias[:, :, None], (items, width, 4)).reshape(items, width * 4)
    stat_a = doubled(doubled(stat[:, :2], 2), 1)
    stat_b = doubled(doubled(stat[:, 2:], 1), 2)
    softmax = attend(target, query, bias, send)
    softmax = score(ORDERS, place, target, stat_a, stat_b, send, softmax)
    parts = exchange(after(softmax, arrived))
    packed = put_blocks(place, target, arrived)
    share, scores = combine(place, target, after(parts, packed), query)
    attended = exchange(share)
    decoded = lax.psum(finish(attended, w_out), "head").astype(BF)
    return packed.reshape(requests, lists * width, local_kv, pair), scores, decoded


def joined(value, axis, join):
    pieces = jax.tree.map(lambda part: lax.all_gather(part, axis), value)
    head = jax.tree.map(lambda part: part[0], pieces)
    tail = jax.tree.map(lambda part: part[1:], pieces)
    running, _ = lax.scan(lambda running, share: (join(running, share), None), head, tail)
    return running


def group_scores(keys, mean_q, cov_q):
    lifted = keys.astype(jnp.float32)
    linear = jnp.einsum("nkd,kgd->nkg", lifted, mean_q, precision=HIGHEST)
    turned = jnp.einsum("nkd,kgde->nkge", lifted, cov_q, precision=HIGHEST)
    quadratic = jnp.sum(turned * lifted[:, :, None, :], axis=-1)
    logits = linear / math.sqrt(keys.shape[-1]) + quadratic / (2.0 * keys.shape[-1])
    top = jnp.max(logits, axis=2)
    return top + jnp.log(jnp.mean(jnp.exp(logits - top[:, :, None]), axis=2))


def combine_parts(first, second):
    top_a, total_a, weighted_a = first
    top_b, total_b, weighted_b = second
    best = jnp.maximum(top_a, top_b)
    factor_a = jnp.exp(top_a - best)
    factor_b = jnp.exp(top_b - best)
    return (
        best,
        total_a * factor_a + total_b * factor_b,
        weighted_a * factor_a[..., None] + weighted_b * factor_b[..., None],
    )


def moments(sample):
    second = jnp.einsum("rshd,rshe->rhde", sample, sample, preferred_element_type=jnp.float32)
    summed = jnp.sum(sample.astype(jnp.float32), axis=1)
    return (second, summed)


KVH = 8


def per_device(
    kv_cache, keep_rows, block_target, future_queries, new_tokens, w_query, w_keyval, w_out
):
    requests, cache_rows, local_kv, pair = kv_cache.shape
    head_size = pair // 2
    lists, width = (keep_rows.shape[1], keep_rows.shape[2])
    span = 2 * width
    group = H // KVH
    ctx_count = lax.axis_size("ctx")
    position = lax.axis_index("ctx")
    root_size = math.sqrt(head_size)
    sample = future_queries.reshape(requests, -1, local_kv * group, head_size)
    second, summed = moments(sample)
    second, summed = lax.psum((second, summed), "ctx")
    mean_q = summed / QS
    cov_q = second / QS - mean_q[..., :, None] * mean_q[..., None, :]
    mean_q = mean_q.reshape(requests, local_kv, group, head_size)
    cov_q = cov_q.reshape(requests, local_kv, group, head_size, head_size)
    span_index = jnp.arange(span, dtype=jnp.int32)
    block_kv, block_score, block_count = ([], [], [])
    for request in range(requests):
        listed = keep_rows[request]
        picker = (listed[:, :, None] == span_index[None, None, :]).astype(jnp.bfloat16)
        spans = kv_cache[request].reshape(lists, span, local_kv * pair)
        chosen = jnp.einsum(
            "bjs,bsc->bjc", picker, spans, preferred_element_type=jnp.float32
        ).astype(jnp.bfloat16)
        chosen = chosen.reshape(lists, width, local_kv, pair)
        every = group_scores(kv_cache[request][:, :, :head_size], mean_q[request], cov_q[request])
        every = every.reshape(lists, span, local_kv)
        picked = jnp.einsum("bjs,bsk->bkj", picker.astype(jnp.float32), every, precision=HIGHEST)
        block_kv.append(chosen)
        block_score.append(picked)
        block_count.append(jnp.sum((listed < span).astype(jnp.int32), axis=1))
    items_kv = jnp.concatenate(block_kv, axis=0)
    items_score = jnp.concatenate(block_score, axis=0)
    items_count = jnp.concatenate(block_count, axis=0)
    total_items = requests * lists
    targets = block_target.reshape(total_items, 2)
    offset = (targets[:, 0] - position) % ctx_count
    slot = targets[:, 1].reshape(requests, lists)
    peers = jnp.arange(ctx_count, dtype=jnp.int32)
    outgoing = targets[:, 0][None, :] == peers[:, None]
    send_kv = jnp.einsum(
        "pm,mjkc->pjkc", outgoing.astype(jnp.bfloat16), items_kv, preferred_element_type=jnp.float32
    ).astype(jnp.bfloat16)
    send_score = jnp.einsum(
        "pm,mkj->pkj", outgoing.astype(jnp.float32), items_score, precision=HIGHEST
    )
    send_count = jnp.sum(jnp.where(outgoing, items_count[None, :], 0), axis=1)
    recv_kv, recv_score, recv_count = (
        lax.all_to_all(send_kv, "ctx", split_axis=0, concat_axis=0, tiled=True),
        lax.all_to_all(
            send_score.astype(jnp.bfloat16), "ctx", split_axis=0, concat_axis=0, tiled=True
        ).astype(send_score.dtype),
        lax.all_to_all(send_count, "ctx", split_axis=0, concat_axis=0, tiled=True),
    )
    source = (position - offset) % ctx_count
    incoming = source[:, None] == peers[None, :]
    got_kv = jnp.einsum(
        "mp,pjkc->mjkc", incoming.astype(jnp.bfloat16), recv_kv, preferred_element_type=jnp.float32
    ).astype(jnp.bfloat16)
    got_score = jnp.einsum(
        "mp,pkj->mkj", incoming.astype(jnp.float32), recv_score, precision=HIGHEST
    )
    got_count = jnp.sum(jnp.where(incoming, recv_count[None, :], 0), axis=1)
    slot_table = slot[:, None, :] == jnp.arange(lists, dtype=jnp.int32)[None, :, None]
    placed_kv = jnp.einsum(
        "rsb,rbjkc->rsjkc",
        slot_table.astype(jnp.bfloat16),
        got_kv.reshape(requests, lists, width, local_kv, pair),
        preferred_element_type=jnp.float32,
    ).astype(jnp.bfloat16)
    packed_cache = placed_kv.reshape(requests, lists * width, local_kv, pair)
    placed_score = jnp.einsum(
        "rsb,rbkj->rksj",
        slot_table.astype(jnp.float32),
        got_score.reshape(requests, lists, local_kv, width),
        precision=HIGHEST,
    )
    packed_scores = placed_score.reshape(requests, local_kv, lists * width)
    placed_count = jnp.sum(jnp.where(slot_table, got_count.reshape(requests, 1, lists), 0), axis=2)
    live = (jnp.arange(width, dtype=jnp.int32)[None, None, :] < placed_count[:, :, None]).reshape(
        requests, lists * width
    )
    steps = new_tokens.shape[0]
    local_width = new_tokens.shape[2]
    flat = new_tokens.reshape(steps * requests, local_width)
    wide = flat.astype(jnp.float32)
    squares = jnp.sum(wide * wide, axis=1)
    query_part = jnp.dot(flat, w_query, preferred_element_type=jnp.float32)
    pair_part = jnp.dot(
        flat, w_keyval.reshape(local_width, local_kv * pair), preferred_element_type=jnp.float32
    )
    squares, query_part, pair_part = lax.psum((squares, query_part, pair_part), "ctx")
    inverse = lax.rsqrt(squares / D + EPSILON)
    query = (
        (query_part * inverse[:, None])
        .astype(jnp.bfloat16)
        .reshape(steps, requests, local_kv, group, head_size)
    )
    fresh = (
        (pair_part * inverse[:, None]).astype(jnp.bfloat16).reshape(steps, requests, local_kv, pair)
    )
    query = jnp.transpose(query, (1, 2, 0, 3, 4)).reshape(
        requests, local_kv, steps * group, head_size
    )
    fresh = jnp.transpose(fresh, (1, 2, 0, 3))
    logits = (
        jnp.einsum(
            "rkqd,rnkd->rkqn",
            query,
            packed_cache[..., :head_size],
            preferred_element_type=jnp.float32,
        )
        / root_size
    )
    logits = jnp.where(live[:, None, None, :], logits, -jnp.inf)
    top = jnp.max(logits, axis=3)
    weights = jnp.exp(logits - top[..., None])
    totals = jnp.sum(weights, axis=3)
    weighted = jnp.einsum(
        "rkqn,rnkd->rkqd",
        weights.astype(jnp.bfloat16),
        packed_cache[..., head_size:],
        preferred_element_type=jnp.float32,
    )
    top, totals, weighted = joined((top, totals, weighted), "ctx", combine_parts)
    recent = (
        jnp.einsum(
            "rkqd,rkud->rkqu", query, fresh[..., :head_size], preferred_element_type=jnp.float32
        )
        / root_size
    )
    causal = (jnp.arange(steps * group, dtype=jnp.int32) // group)[:, None] >= jnp.arange(
        steps, dtype=jnp.int32
    )[None, :]
    recent = jnp.where(causal[None, None], recent, -jnp.inf)
    best = jnp.maximum(top, jnp.max(recent, axis=3))
    weight_new = jnp.exp(recent - best[..., None])
    factor_old = jnp.exp(top - best)
    normalizer = totals * factor_old + jnp.sum(weight_new, axis=3)
    weighted = weighted * factor_old[..., None] + jnp.einsum(
        "rkqu,rkud->rkqd",
        weight_new.astype(jnp.bfloat16),
        fresh[..., head_size:],
        preferred_element_type=jnp.float32,
    )
    attended = (weighted / normalizer[..., None]).astype(jnp.bfloat16)
    attended = attended.reshape(requests, local_kv, steps, group, head_size)
    attended = jnp.transpose(attended, (2, 0, 1, 3, 4)).reshape(
        steps * requests, local_kv * group * head_size
    )
    partial_value = jnp.dot(attended, w_out, preferred_element_type=jnp.float32)
    summed_out = lax.psum(partial_value, "head")
    decoded = summed_out.astype(jnp.bfloat16).reshape(steps, requests, local_width)
    return (packed_cache, packed_scores, decoded)


def solution(mesh):
    in_specs = (
        P(None, "ctx", "head", None),
        P(None, "ctx", None),
        P(None, "ctx", None),
        P(None, "ctx", "head"),
        P(None, None, "ctx"),
        P("ctx", "head"),
        P("ctx", "head", None),
        P("head", "ctx"),
    )
    out_specs = (P(None, "ctx", "head", None), P(None, "head", "ctx"), P(None, None, "ctx"))
    body = sixteen if mesh.shape["ctx"] == 16 and mesh.shape["head"] == 2 else per_device
    return jax.shard_map(
        body, mesh=mesh, in_specs=in_specs, out_specs=out_specs, check_vma=False
    )
```

```python
import math

import jax
import jax.numpy as jnp
from jax import lax
from jax.experimental import pallas as pl
from jax.experimental.pallas import tpu as pltpu
from jax.sharding import PartitionSpec as P

D = 8192
H = 64
QS = 256
EPSILON = 1e-05
HIGHEST = lax.Precision.HIGHEST
BF = jnp.bfloat16
F32 = jnp.float32
STAT = 144
LARGE = 1e30
ANY = pl.BlockSpec(memory_space=pltpu.HBM)
SMEM = pl.BlockSpec(memory_space=pltpu.SMEM)
VMEM = pl.BlockSpec(memory_space=pltpu.VMEM)
NT = (((1,), (1,)), ((), ()))
TN = (((0,), (0,)), ((), ()))


def hbm(value):
    return pltpu.with_memory_space_constraint(value, pltpu.HBM)


def params(megabytes=8):
    return pltpu.CompilerParams(vmem_limit_bytes=megabytes << 20)


def pack_kernel(keep, target, kv, send, spans, blocks, in_sem, out_sem):
    items, width = keep.shape
    span = 2 * width
    lists = items // kv.shape[0]

    def fetch(m):
        return pltpu.make_async_copy(
            kv.at[m // lists, pl.ds((m % lists) * span, span)], spans.at[m, pl.ds(0, span)], in_sem.at[m]
        )

    def put(m):
        return pltpu.make_async_copy(blocks.at[m], send.at[target[m, 0]], out_sem.at[m])

    for m in range(items):
        fetch(m).start()
        spans[m, span] = jnp.zeros(spans.shape[2:], spans.dtype)

    def one(m, carry):
        fetch(m).wait()

        def rows(j, inner):
            values = [spans[m, keep[m, j * 16 + u]] for u in range(16)]
            for u in range(16):
                blocks[m, j * 16 + u] = values[u]
            return inner

        lax.fori_loop(0, width // 16, rows, 0)
        put(m).start()
        return carry

    lax.fori_loop(0, items, one, 0)
    for m in range(items):
        put(m).wait()


def pack(kv_cache, keep, target):
    items, width = keep.shape
    tail = kv_cache.shape[2:]
    return pl.pallas_call(
        pack_kernel,
        out_shape=pltpu.HBM((items, width, *tail), kv_cache.dtype),
        in_specs=[SMEM, SMEM, ANY],
        out_specs=ANY,
        scratch_shapes=[
            pltpu.VMEM((items, 2 * width + 8, *tail), kv_cache.dtype),
            pltpu.VMEM((items, width, *tail), kv_cache.dtype),
            pltpu.SemaphoreType.DMA((items,)),
            pltpu.SemaphoreType.DMA((items,)),
        ],
        compiler_params=params(20),
        name="pack_rows",
    )(keep, target, hbm(kv_cache))


def split_kernel(samples, out):
    for r in range(2):
        for c in range(32):
            out[r * 8 + c // 4, (c % 4) * 16 : (c % 4) * 16 + 16, :] = samples[
                r, :, c * 128 : c * 128 + 128
            ]


def split_samples(samples):
    return pl.pallas_call(
        split_kernel,
        out_shape=jax.ShapeDtypeStruct((16, 64, 128), BF),
        in_specs=[VMEM],
        out_specs=VMEM,
        compiler_params=params(),
        name="split_samples",
    )(samples)


def project_kernel(tokens, wq, wkv, out):
    i = pl.program_id(0)
    x = jnp.concatenate([tokens[t, r : r + 1, :].astype(F32) for r in range(2) for t in range(4)], axis=0)
    x = x.astype(BF)
    part = jnp.dot(x, wq[...], preferred_element_type=F32)
    for r in range(2):
        for g in range(8):
            out[r * 8 + i * 2 + g // 4, (g % 4) * 4 : (g % 4) * 4 + 4, :] = part[
                r * 4 : r * 4 + 4, g * 128 : g * 128 + 128
            ]

    @pl.when(i == 0)
    def _():
        heads = pltpu.einshape("nhd->hnd", wkv[...])
        wide = x.astype(F32)
        squares = jnp.sum(wide * wide, axis=1, keepdims=True)
        row = lax.broadcasted_iota(jnp.int32, (8, 128), 0)
        lane = lax.broadcasted_iota(jnp.int32, (8, 128), 1)
        line = jnp.sum(jnp.where(row == lane, squares, 0.0), axis=0, keepdims=True)
        line = jnp.concatenate([line, jnp.zeros((3, 128), F32)], axis=0)
        for p in range(16):
            out[p, 20:24, :] = line
        for j in range(4):
            pair = jnp.dot(x, heads[j], preferred_element_type=F32)
            for r in range(2):
                for half in range(2):
                    out[r * 8 + j * 2 + half, 16:20, :] = pair[
                        r * 4 : r * 4 + 4, half * 128 : half * 128 + 128
                    ]


def project(tokens, w_query, w_keyval):
    depth, columns = w_query.shape
    step = columns // 4
    return pl.pallas_call(
        project_kernel,
        out_shape=jax.ShapeDtypeStruct((16, 24, 128), F32),
        grid=(4,),
        in_specs=[
            pl.BlockSpec(tokens.shape, lambda i: (0, 0, 0)),
            pl.BlockSpec((depth, step), lambda i: (0, i)),
            pl.BlockSpec(w_keyval.shape, lambda i: (0, 0, 0)),
        ],
        out_specs=pl.BlockSpec((16, 24, 128), lambda i: (0, 0, 0)),
        compiler_params=params(16),
        name="project_tokens",
    )(hbm(tokens), hbm(w_query), hbm(w_keyval))


def normalize_kernel(place, parts, out):
    total = jnp.sum(parts[...], axis=0)
    request = place[0] // 8
    row = lax.broadcasted_iota(jnp.int32, (24, 128), 0)
    lane = lax.broadcasted_iota(jnp.int32, (24, 128), 1)
    squares = jnp.where(lane == request * 4 + row % 4, total[20:21, :], 0.0)
    inverse = lax.rsqrt(jnp.sum(squares, axis=1, keepdims=True) / D + EPSILON)
    scaled = jnp.where(row < 20, total * inverse, 0.0)
    rounded = jnp.concatenate([scaled, jnp.zeros((8, 128), F32)], axis=0).astype(BF)
    out[...] = jnp.broadcast_to(rounded[None], out.shape)


def normalize(place, parts):
    return pl.pallas_call(
        normalize_kernel,
        out_shape=jax.ShapeDtypeStruct((16, 32, 128), BF),
        in_specs=[SMEM, VMEM],
        out_specs=VMEM,
        compiler_params=params(),
        name="normalize_tokens",
    )(place, parts)


def moments_kernel(parts, stat):
    for i in range(4):
        q = parts[:, i * 16 : i * 16 + 16, :].reshape(256, 128)
        second = lax.dot_general(q, q, TN, preferred_element_type=F32)
        mean = jnp.sum(q.astype(F32), axis=0, keepdims=True) / QS
        first = jnp.concatenate([mean, jnp.zeros((7, 128), F32)], axis=0)
        outer = lax.dot_general(first, first, TN, preferred_element_type=F32, precision=HIGHEST)
        cov = second / QS - outer
        scaled = mean / math.sqrt(128)
        high = scaled.astype(BF).astype(F32)
        lines = jnp.concatenate([high, scaled - high, jnp.zeros((14, 128), F32)], axis=0)
        stat[0, i, 0:128, :] = cov.astype(BF)
        stat[0, i, 128:144, :] = lines.astype(BF)


def head_moments(parts):
    return pl.pallas_call(
        moments_kernel,
        out_shape=jax.ShapeDtypeStruct((1, 4, STAT, 128), BF),
        in_specs=[VMEM],
        out_specs=VMEM,
        compiler_params=params(),
        name="head_moments",
    )(parts)


def attend_kernel(target, query, bias, send, out, rows, logits, sem):
    items = rows.shape[0]
    width = rows.shape[1]
    wide = width * 4

    def fetch(m):
        return pltpu.make_async_copy(send.at[target[m, 0]], rows.at[m], sem.at[m])

    for m in range(items):
        fetch(m).start()
    head = lax.broadcasted_iota(jnp.int32, (128, wide), 0) // 32
    lane = lax.broadcasted_iota(jnp.int32, (128, wide), 1) % 4
    own = head == lane
    for r in range(2):
        q = query[r * 8 : r * 8 + 8, 0:16, :].reshape(128, 128)
        for b in range(8):
            m = r * 8 + b
            fetch(m).wait()
            keys = rows[m, :, :, 0:128].reshape(wide, 128)
            scores = lax.dot_general(q, keys, NT, preferred_element_type=F32) / math.sqrt(128)
            scores = jnp.where(own, scores, -LARGE) + bias[m : m + 1, :]
            logits[:, b * wide : b * wide + wide] = scores
        top = jnp.max(logits[...], axis=1, keepdims=True)
        total = jnp.zeros((128, 1), F32)
        weighted = jnp.zeros((128, 128), F32)
        for b in range(8):
            weights = jnp.exp(logits[:, b * wide : b * wide + wide] - top)
            total = total + jnp.sum(weights, axis=1, keepdims=True)
            values = rows[r * 8 + b, :, :, 128:256].reshape(wide, 128)
            weighted = weighted + jnp.dot(weights.astype(BF), values, preferred_element_type=F32)
        top_line = jnp.broadcast_to(top, (128, 128)).T[0:1, :]
        total_line = jnp.broadcast_to(total, (128, 128)).T[0:1, :]
        lines = jnp.concatenate([top_line, total_line, jnp.zeros((6, 128), F32)], axis=0)
        for i in range(8):
            out[r * 8 + i, 0:16, :] = weighted[i * 16 : i * 16 + 16, :]
            out[r * 8 + i, 16:24, :] = lines


def attend(target, query, bias, send):
    items, width = send.shape[:2]
    return pl.pallas_call(
        attend_kernel,
        out_shape=jax.ShapeDtypeStruct((16, 24, 128), F32),
        in_specs=[SMEM, VMEM, VMEM, ANY],
        out_specs=VMEM,
        scratch_shapes=[
            pltpu.VMEM(send.shape, send.dtype),
            pltpu.VMEM((128, 8 * width * 4), F32),
            pltpu.SemaphoreType.DMA((items,)),
        ],
        compiler_params=params(16),
        name="attend_kept",
    )(target, query, bias, hbm(send))


def combine_kernel(place, target, parts, query, out, scores):
    p = place[0]
    mine = query[p, 0:16, :]
    pair = (p // 2) * 2
    fresh_key = query[pair, 16:32, :]
    fresh_value = query[pair + 1, 16:32, :]
    recent = lax.dot_general(mine, fresh_key, NT, preferred_element_type=F32) / math.sqrt(128)
    step = lax.broadcasted_iota(jnp.int32, (16, 16), 0) % 4
    column = lax.broadcasted_iota(jnp.int32, (16, 16), 1)
    recent = jnp.where(column <= step, recent, -LARGE)
    row = lax.broadcasted_iota(jnp.int32, (16, 128), 0)
    lane = lax.broadcasted_iota(jnp.int32, (16, 128), 1)
    chosen = lane == (p % 8) * 16 + row
    tops, totals = [], []
    for s in range(16):
        tops.append(jnp.sum(jnp.where(chosen, parts[s, 16:17, :], 0.0), axis=1, keepdims=True))
        totals.append(jnp.sum(jnp.where(chosen, parts[s, 17:18, :], 0.0), axis=1, keepdims=True))
    best = jnp.max(recent, axis=1, keepdims=True)
    for s in range(16):
        best = jnp.maximum(best, tops[s])
    weights = jnp.exp(recent - best)
    total = jnp.sum(weights, axis=1, keepdims=True)
    weighted = jnp.dot(weights.astype(BF), fresh_value, preferred_element_type=F32)
    for s in range(16):
        factor = jnp.exp(tops[s] - best)
        total = total + totals[s] * factor
        weighted = weighted + parts[s, 0:16, :] * factor
    out[...] = jnp.broadcast_to((weighted / total).astype(BF)[None], out.shape)
    for m in range(16):
        start = pl.multiple_of(target[m, 1] * 128, 128)
        scores[m // 8, :, pl.ds(start, 128)] = parts[sender(m, p, target, 16), 18:22, :]


def combine(place, target, parts, query):
    return pl.pallas_call(
        combine_kernel,
        out_shape=(
            jax.ShapeDtypeStruct((16, 16, 128), BF),
            jax.ShapeDtypeStruct((2, 4, 1024), F32),
        ),
        in_specs=[SMEM, SMEM, VMEM, VMEM],
        out_specs=(VMEM, VMEM),
        compiler_params=params(),
        name="combine_parts",
    )(place, target, parts, query)


def reverse_bits(value, order):
    place = 0
    for at, bit in enumerate(order):
        place = place + ((value // bit) % 2) * (1 << at)
    return place


def score_kernel(orders, place, target, stat_a, stat_b, send, parts, out, blocks, sem):
    items = blocks.shape[0]
    lists = items // 2
    me = place[0]

    def fetch(m):
        return pltpu.make_async_copy(send.at[target[m, 0]], blocks.at[m], sem.at[m])

    for m in range(items):
        fetch(m).start()
    out[...] = parts[...]
    for m in range(items):
        fetch(m).wait()
    for r in range(2):
        for j in range(4):
            tables = []
            for o in range(2):
                owner = jnp.bitwise_xor(me, r * 8 + j * 2 + o)
                for half, stat in enumerate((stat_a, stat_b)):
                    tables.append(stat[reverse_bits(owner, orders[half])].reshape(2 * STAT, 128))
            table = jnp.concatenate(tables, axis=0)
            for c in range(lists // 2):
                first = r * lists + c * 2
                keys = blocks[first : first + 2, :, j, 0:128].reshape(256, 128)
                turned_keys = keys.T
                flipped = turned_keys.astype(F32)
                logits = []
                turned = jnp.dot(table, turned_keys, preferred_element_type=F32)
                for g in range(8):
                    base = g * STAT
                    quadratic = jnp.sum(turned[base : base + 128] * flipped, axis=0, keepdims=True)
                    linear = turned[base + 128 : base + 129] + turned[base + 129 : base + 130]
                    logits.append(linear + quadratic / 256.0)
                logit = jnp.concatenate(logits, axis=0)
                top = jnp.max(logit, axis=0, keepdims=True)
                mean = jnp.sum(jnp.exp(logit - top), axis=0, keepdims=True) / 8.0
                line = top + jnp.log(mean)
                for u in range(2):
                    p = target[first + u, 0]
                    out[p, 18 + j : 19 + j, :] = line[:, u * 128 : u * 128 + 128]


def score(orders, place, target, stat_a, stat_b, send, parts):
    items = send.shape[0]

    def kernel(*refs):
        score_kernel(orders, *refs)

    return pl.pallas_call(
        kernel,
        out_shape=jax.ShapeDtypeStruct(parts.shape, parts.dtype),
        in_specs=[SMEM, SMEM, VMEM, VMEM, ANY, VMEM],
        out_specs=VMEM,
        scratch_shapes=[
            pltpu.VMEM(send.shape, send.dtype),
            pltpu.SemaphoreType.DMA((items,)),
        ],
        compiler_params=params(24),
        name="score_kept",
    )(place, target, stat_a, stat_b, hbm(send), parts)


def sender(m, me, target, count):
    return (2 * me - target[m, 0] + count) % count


def place_kernel(place, target, arrived, packed, blocks, in_sem, out_sem):
    items = arrived.shape[0]
    lists = items // 2

    def fetch(m):
        return pltpu.make_async_copy(
            arrived.at[sender(m, place[0], target, items)], blocks.at[m], in_sem.at[m]
        )

    def put(m):
        slot = (m // lists) * lists + target[m, 1]
        return pltpu.make_async_copy(blocks.at[m], packed.at[slot], out_sem.at[m])

    for m in range(items):
        fetch(m).start()
    for m in range(items):
        fetch(m).wait()
        put(m).start()
    for m in range(items):
        put(m).wait()


def put_blocks(place, target, arrived):
    items = arrived.shape[0]
    return pl.pallas_call(
        place_kernel,
        out_shape=pltpu.HBM(arrived.shape, arrived.dtype),
        in_specs=[SMEM, SMEM, ANY],
        out_specs=ANY,
        scratch_shapes=[
            pltpu.VMEM(arrived.shape, arrived.dtype),
            pltpu.SemaphoreType.DMA((items,)),
            pltpu.SemaphoreType.DMA((items,)),
        ],
        compiler_params=params(),
        name="place_blocks",
    )(place, target, hbm(arrived))


def finish_kernel(joined, w, out, rows, weight, sem):
    quarter = w.shape[0] // 4

    def fetch(i):
        part = pl.ds(i * quarter, quarter)
        return pltpu.make_async_copy(w.at[part], weight.at[part], sem.at[i])

    for i in range(4):
        fetch(i).start()
    for r in range(2):
        for h in range(32):
            at = (h % 4) * 4
            rows[r * 4 : r * 4 + 4, h * 128 : h * 128 + 128] = joined[
                r * 8 + h // 4, at : at + 4, :
            ].astype(F32)
    value = jnp.zeros((8, w.shape[1]), F32)
    for i in range(4):
        fetch(i).wait()
        part = slice(i * quarter, i * quarter + quarter)
        value = value + jnp.dot(
            rows[:, part].astype(BF), weight[part, :], preferred_element_type=F32
        )
    for r in range(2):
        for t in range(4):
            out[t, r : r + 1, :] = value[r * 4 + t : r * 4 + t + 1, :]


def finish(joined, w_out):
    return pl.pallas_call(
        finish_kernel,
        out_shape=jax.ShapeDtypeStruct((4, 2, w_out.shape[1]), F32),
        in_specs=[VMEM, ANY],
        out_specs=VMEM,
        scratch_shapes=[
            pltpu.VMEM((8, w_out.shape[0]), F32),
            pltpu.VMEM(w_out.shape, w_out.dtype),
            pltpu.SemaphoreType.DMA((4,)),
        ],
        compiler_params=params(),
        name="project_out",
    )(joined, hbm(w_out))


def exchange(value):
    return lax.all_to_all(value, "ctx", split_axis=0, concat_axis=0, tiled=True)


def doubled(value, bit):
    pairs = [(i, i ^ bit) for i in range(16)]
    return jnp.concatenate([value, lax.ppermute(value, "ctx", pairs)], axis=0)


def after(values, token):
    return lax.optimization_barrier((values, token))[0]


ORDERS = ((8, 4, 2, 1), (8, 4, 1, 2))


def sixteen(
    kv_cache, keep_rows, block_target, future_queries, new_tokens, w_query, w_keyval, w_out
):
    requests, cache_rows, local_kv, pair = kv_cache.shape
    lists, width = keep_rows.shape[1:]
    items = requests * lists
    keep = keep_rows.reshape(items, width)
    target = block_target.reshape(items, 2)
    place = lax.axis_index("ctx").astype(jnp.int32).reshape(1)
    samples = exchange(split_samples(future_queries))
    parts, samples = lax.optimization_barrier((project(new_tokens, w_query, w_keyval), samples))
    parts = exchange(parts)
    stat = doubled(head_moments(samples), 8)
    send = pack(kv_cache, after(keep, samples), target)
    stat = doubled(after(stat, send), 4)
    query = exchange(normalize(place, after(parts, send)))
    arrived = exchange(after(send, (query, stat)))
    bias = jnp.where(after(keep, query) < 2 * width, 0.0, -LARGE).astype(F32)
    bias = jnp.broadcast_to(bias[:, :, None], (items, width, 4)).reshape(items, width * 4)
    stat_a = doubled(doubled(stat[:, :2], 2), 1)
    stat_b = doubled(doubled(stat[:, 2:], 1), 2)
    softmax = attend(target, query, bias, send)
    softmax = score(ORDERS, place, target, stat_a, stat_b, send, softmax)
    parts = exchange(after(softmax, arrived))
    packed = put_blocks(place, target, arrived)
    share, scores = combine(place, target, after(parts, packed), query)
    attended = exchange(share)
    decoded = lax.psum(finish(attended, w_out), "head").astype(BF)
    return packed.reshape(requests, lists * width, local_kv, pair), scores, decoded


def joined(value, axis, join):
    pieces = jax.tree.map(lambda part: lax.all_gather(part, axis), value)
    head = jax.tree.map(lambda part: part[0], pieces)
    tail = jax.tree.map(lambda part: part[1:], pieces)
    running, _ = lax.scan(lambda running, share: (join(running, share), None), head, tail)
    return running


def group_scores(keys, mean_q, cov_q):
    lifted = keys.astype(jnp.float32)
    linear = jnp.einsum("nkd,kgd->nkg", lifted, mean_q, precision=HIGHEST)
    turned = jnp.einsum("nkd,kgde->nkge", lifted, cov_q, precision=HIGHEST)
    quadratic = jnp.sum(turned * lifted[:, :, None, :], axis=-1)
    logits = linear / math.sqrt(keys.shape[-1]) + quadratic / (2.0 * keys.shape[-1])
    top = jnp.max(logits, axis=2)
    return top + jnp.log(jnp.mean(jnp.exp(logits - top[:, :, None]), axis=2))


def combine_parts(first, second):
    top_a, total_a, weighted_a = first
    top_b, total_b, weighted_b = second
    best = jnp.maximum(top_a, top_b)
    factor_a = jnp.exp(top_a - best)
    factor_b = jnp.exp(top_b - best)
    return (
        best,
        total_a * factor_a + total_b * factor_b,
        weighted_a * factor_a[..., None] + weighted_b * factor_b[..., None],
    )


def moments(sample):
    second = jnp.einsum("rshd,rshe->rhde", sample, sample, preferred_element_type=jnp.float32)
    summed = jnp.sum(sample.astype(jnp.float32), axis=1)
    return (second, summed)


KVH = 8


def per_device(
    kv_cache, keep_rows, block_target, future_queries, new_tokens, w_query, w_keyval, w_out
):
    requests, cache_rows, local_kv, pair = kv_cache.shape
    head_size = pair // 2
    lists, width = (keep_rows.shape[1], keep_rows.shape[2])
    span = 2 * width
    group = H // KVH
    ctx_count = lax.axis_size("ctx")
    position = lax.axis_index("ctx")
    root_size = math.sqrt(head_size)
    sample = future_queries.reshape(requests, -1, local_kv * group, head_size)
    second, summed = moments(sample)
    second, summed = lax.psum((second, summed), "ctx")
    mean_q = summed / QS
    cov_q = second / QS - mean_q[..., :, None] * mean_q[..., None, :]
    mean_q = mean_q.reshape(requests, local_kv, group, head_size)
    cov_q = cov_q.reshape(requests, local_kv, group, head_size, head_size)
    span_index = jnp.arange(span, dtype=jnp.int32)
    block_kv, block_score, block_count = ([], [], [])
    for request in range(requests):
        listed = keep_rows[request]
        picker = (listed[:, :, None] == span_index[None, None, :]).astype(jnp.bfloat16)
        spans = kv_cache[request].reshape(lists, span, local_kv * pair)
        chosen = jnp.einsum(
            "bjs,bsc->bjc", picker, spans, preferred_element_type=jnp.float32
        ).astype(jnp.bfloat16)
        chosen = chosen.reshape(lists, width, local_kv, pair)
        every = group_scores(kv_cache[request][:, :, :head_size], mean_q[request], cov_q[request])
        every = every.reshape(lists, span, local_kv)
        picked = jnp.einsum("bjs,bsk->bkj", picker.astype(jnp.float32), every, precision=HIGHEST)
        block_kv.append(chosen)
        block_score.append(picked)
        block_count.append(jnp.sum((listed < span).astype(jnp.int32), axis=1))
    items_kv = jnp.concatenate(block_kv, axis=0)
    items_score = jnp.concatenate(block_score, axis=0)
    items_count = jnp.concatenate(block_count, axis=0)
    total_items = requests * lists
    targets = block_target.reshape(total_items, 2)
    offset = (targets[:, 0] - position) % ctx_count
    slot = targets[:, 1].reshape(requests, lists)
    peers = jnp.arange(ctx_count, dtype=jnp.int32)
    outgoing = targets[:, 0][None, :] == peers[:, None]
    send_kv = jnp.einsum(
        "pm,mjkc->pjkc", outgoing.astype(jnp.bfloat16), items_kv, preferred_element_type=jnp.float32
    ).astype(jnp.bfloat16)
    send_score = jnp.einsum(
        "pm,mkj->pkj", outgoing.astype(jnp.float32), items_score, precision=HIGHEST
    )
    send_count = jnp.sum(jnp.where(outgoing, items_count[None, :], 0), axis=1)
    recv_kv, recv_score, recv_count = (
        lax.all_to_all(send_kv, "ctx", split_axis=0, concat_axis=0, tiled=True),
        lax.all_to_all(
            send_score.astype(jnp.bfloat16), "ctx", split_axis=0, concat_axis=0, tiled=True
        ).astype(send_score.dtype),
        lax.all_to_all(send_count, "ctx", split_axis=0, concat_axis=0, tiled=True),
    )
    source = (position - offset) % ctx_count
    incoming = source[:, None] == peers[None, :]
    got_kv = jnp.einsum(
        "mp,pjkc->mjkc", incoming.astype(jnp.bfloat16), recv_kv, preferred_element_type=jnp.float32
    ).astype(jnp.bfloat16)
    got_score = jnp.einsum(
        "mp,pkj->mkj", incoming.astype(jnp.float32), recv_score, precision=HIGHEST
    )
    got_count = jnp.sum(jnp.where(incoming, recv_count[None, :], 0), axis=1)
    slot_table = slot[:, None, :] == jnp.arange(lists, dtype=jnp.int32)[None, :, None]
    placed_kv = jnp.einsum(
        "rsb,rbjkc->rsjkc",
        slot_table.astype(jnp.bfloat16),
        got_kv.reshape(requests, lists, width, local_kv, pair),
        preferred_element_type=jnp.float32,
    ).astype(jnp.bfloat16)
    packed_cache = placed_kv.reshape(requests, lists * width, local_kv, pair)
    placed_score = jnp.einsum(
        "rsb,rbkj->rksj",
        slot_table.astype(jnp.float32),
        got_score.reshape(requests, lists, local_kv, width),
        precision=HIGHEST,
    )
    packed_scores = placed_score.reshape(requests, local_kv, lists * width)
    placed_count = jnp.sum(jnp.where(slot_table, got_count.reshape(requests, 1, lists), 0), axis=2)
    live = (jnp.arange(width, dtype=jnp.int32)[None, None, :] < placed_count[:, :, None]).reshape(
        requests, lists * width
    )
    steps = new_tokens.shape[0]
    local_width = new_tokens.shape[2]
    flat = new_tokens.reshape(steps * requests, local_width)
    wide = flat.astype(jnp.float32)
    squares = jnp.sum(wide * wide, axis=1)
    query_part = jnp.dot(flat, w_query, preferred_element_type=jnp.float32)
    pair_part = jnp.dot(
        flat, w_keyval.reshape(local_width, local_kv * pair), preferred_element_type=jnp.float32
    )
    squares, query_part, pair_part = lax.psum((squares, query_part, pair_part), "ctx")
    inverse = lax.rsqrt(squares / D + EPSILON)
    query = (
        (query_part * inverse[:, None])
        .astype(jnp.bfloat16)
        .reshape(steps, requests, local_kv, group, head_size)
    )
    fresh = (
        (pair_part * inverse[:, None]).astype(jnp.bfloat16).reshape(steps, requests, local_kv, pair)
    )
    query = jnp.transpose(query, (1, 2, 0, 3, 4)).reshape(
        requests, local_kv, steps * group, head_size
    )
    fresh = jnp.transpose(fresh, (1, 2, 0, 3))
    logits = (
        jnp.einsum(
            "rkqd,rnkd->rkqn",
            query,
            packed_cache[..., :head_size],
            preferred_element_type=jnp.float32,
        )
        / root_size
    )
    logits = jnp.where(live[:, None, None, :], logits, -jnp.inf)
    top = jnp.max(logits, axis=3)
    weights = jnp.exp(logits - top[..., None])
    totals = jnp.sum(weights, axis=3)
    weighted = jnp.einsum(
        "rkqn,rnkd->rkqd",
        weights.astype(jnp.bfloat16),
        packed_cache[..., head_size:],
        preferred_element_type=jnp.float32,
    )
    top, totals, weighted = joined((top, totals, weighted), "ctx", combine_parts)
    recent = (
        jnp.einsum(
            "rkqd,rkud->rkqu", query, fresh[..., :head_size], preferred_element_type=jnp.float32
        )
        / root_size
    )
    causal = (jnp.arange(steps * group, dtype=jnp.int32) // group)[:, None] >= jnp.arange(
        steps, dtype=jnp.int32
    )[None, :]
    recent = jnp.where(causal[None, None], recent, -jnp.inf)
    best = jnp.maximum(top, jnp.max(recent, axis=3))
    weight_new = jnp.exp(recent - best[..., None])
    factor_old = jnp.exp(top - best)
    normalizer = totals * factor_old + jnp.sum(weight_new, axis=3)
    weighted = weighted * factor_old[..., None] + jnp.einsum(
        "rkqu,rkud->rkqd",
        weight_new.astype(jnp.bfloat16),
        fresh[..., head_size:],
        preferred_element_type=jnp.float32,
    )
    attended = (weighted / normalizer[..., None]).astype(jnp.bfloat16)
    attended = attended.reshape(requests, local_kv, steps, group, head_size)
    attended = jnp.transpose(attended, (2, 0, 1, 3, 4)).reshape(
        steps * requests, local_kv * group * head_size
    )
    partial_value = jnp.dot(attended, w_out, preferred_element_type=jnp.float32)
    summed_out = lax.psum(partial_value, "head")
    decoded = summed_out.astype(jnp.bfloat16).reshape(steps, requests, local_width)
    return (packed_cache, packed_scores, decoded)


def solution(mesh):
    in_specs = (
        P(None, "ctx", "head", None),
        P(None, "ctx", None),
        P(None, "ctx", None),
        P(None, "ctx", "head"),
        P(None, None, "ctx"),
        P("ctx", "head"),
        P("ctx", "head", None),
        P("head", "ctx"),
    )
    out_specs = (P(None, "ctx", "head", None), P(None, "head", "ctx"), P(None, None, "ctx"))
    body = sixteen if mesh.shape["ctx"] == 16 and mesh.shape["head"] == 2 else per_device
    return jax.shard_map(
        body, mesh=mesh, in_specs=in_specs, out_specs=out_specs, check_vma=False
    )
```

```python
import math

import jax
import jax.numpy as jnp
from jax import lax
from jax.experimental import pallas as pl
from jax.experimental.pallas import tpu as pltpu
from jax.sharding import PartitionSpec as P

D = 8192
H = 64
QS = 256
EPSILON = 1e-05
HIGHEST = lax.Precision.HIGHEST
BF = jnp.bfloat16
F32 = jnp.float32
STAT = 144
LARGE = 1e30
ANY = pl.BlockSpec(memory_space=pltpu.HBM)
SMEM = pl.BlockSpec(memory_space=pltpu.SMEM)
VMEM = pl.BlockSpec(memory_space=pltpu.VMEM)
NT = (((1,), (1,)), ((), ()))
TN = (((0,), (0,)), ((), ()))


def hbm(value):
    return pltpu.with_memory_space_constraint(value, pltpu.HBM)


def params(megabytes=8):
    return pltpu.CompilerParams(vmem_limit_bytes=megabytes << 20)


def pack_kernel(keep, target, kv, send, spans, blocks, in_sem, out_sem):
    items, width = keep.shape
    span = 2 * width
    lists = items // kv.shape[0]

    def fetch(m):
        return pltpu.make_async_copy(
            kv.at[m // lists, pl.ds((m % lists) * span, span)], spans.at[m, pl.ds(0, span)], in_sem.at[m]
        )

    def put(m):
        return pltpu.make_async_copy(blocks.at[m], send.at[target[m, 0]], out_sem.at[m])

    for m in range(items):
        fetch(m).start()
        spans[m, span] = jnp.zeros(spans.shape[2:], spans.dtype)

    for m in range(items):
        fetch(m).wait()

        def rows(j, inner):
            values = [spans[m, keep[m, j * 16 + u]] for u in range(16)]
            for u in range(16):
                blocks[m, j * 16 + u] = values[u]
            return inner

        lax.fori_loop(0, width // 16, rows, 0)
        put(m).start()
    for m in range(items):
        put(m).wait()


def pack(kv_cache, keep, target):
    items, width = keep.shape
    tail = kv_cache.shape[2:]
    return pl.pallas_call(
        pack_kernel,
        out_shape=pltpu.HBM((items, width, *tail), kv_cache.dtype),
        in_specs=[SMEM, SMEM, ANY],
        out_specs=ANY,
        scratch_shapes=[
            pltpu.VMEM((items, 2 * width + 8, *tail), kv_cache.dtype),
            pltpu.VMEM((items, width, *tail), kv_cache.dtype),
            pltpu.SemaphoreType.DMA((items,)),
            pltpu.SemaphoreType.DMA((items,)),
        ],
        compiler_params=params(20),
        name="pack_rows",
    )(keep, target, hbm(kv_cache))


def split_kernel(samples, out):
    for r in range(2):
        for c in range(32):
            out[r * 8 + c // 4, (c % 4) * 16 : (c % 4) * 16 + 16, :] = samples[
                r, :, c * 128 : c * 128 + 128
            ]


def split_samples(samples):
    return pl.pallas_call(
        split_kernel,
        out_shape=jax.ShapeDtypeStruct((16, 64, 128), BF),
        in_specs=[VMEM],
        out_specs=VMEM,
        compiler_params=params(),
        name="split_samples",
    )(samples)


def project_kernel(tokens, wq, wkv, out):
    i = pl.program_id(0)
    x = jnp.concatenate([tokens[t, r : r + 1, :].astype(F32) for r in range(2) for t in range(4)], axis=0)
    x = x.astype(BF)
    part = jnp.dot(x, wq[...], preferred_element_type=F32)
    for r in range(2):
        for g in range(8):
            out[r * 8 + i * 2 + g // 4, (g % 4) * 4 : (g % 4) * 4 + 4, :] = part[
                r * 4 : r * 4 + 4, g * 128 : g * 128 + 128
            ]

    @pl.when(i == 0)
    def _():
        heads = pltpu.einshape("nhd->hnd", wkv[...])
        wide = x.astype(F32)
        squares = jnp.sum(wide * wide, axis=1, keepdims=True)
        row = lax.broadcasted_iota(jnp.int32, (8, 128), 0)
        lane = lax.broadcasted_iota(jnp.int32, (8, 128), 1)
        line = jnp.sum(jnp.where(row == lane, squares, 0.0), axis=0, keepdims=True)
        line = jnp.concatenate([line, jnp.zeros((3, 128), F32)], axis=0)
        for p in range(16):
            out[p, 20:24, :] = line
        for j in range(4):
            pair = jnp.dot(x, heads[j], preferred_element_type=F32)
            for r in range(2):
                for half in range(2):
                    out[r * 8 + j * 2 + half, 16:20, :] = pair[
                        r * 4 : r * 4 + 4, half * 128 : half * 128 + 128
                    ]


def project(tokens, w_query, w_keyval):
    depth, columns = w_query.shape
    step = columns // 4
    return pl.pallas_call(
        project_kernel,
        out_shape=jax.ShapeDtypeStruct((16, 24, 128), F32),
        grid=(4,),
        in_specs=[
            pl.BlockSpec(tokens.shape, lambda i: (0, 0, 0)),
            pl.BlockSpec((depth, step), lambda i: (0, i)),
            pl.BlockSpec(w_keyval.shape, lambda i: (0, 0, 0)),
        ],
        out_specs=pl.BlockSpec((16, 24, 128), lambda i: (0, 0, 0)),
        compiler_params=params(16),
        name="project_tokens",
    )(hbm(tokens), hbm(w_query), hbm(w_keyval))


def normalize_kernel(place, parts, out):
    total = jnp.sum(parts[...], axis=0)
    request = place[0] // 8
    row = lax.broadcasted_iota(jnp.int32, (24, 128), 0)
    lane = lax.broadcasted_iota(jnp.int32, (24, 128), 1)
    squares = jnp.where(lane == request * 4 + row % 4, total[20:21, :], 0.0)
    inverse = lax.rsqrt(jnp.sum(squares, axis=1, keepdims=True) / D + EPSILON)
    scaled = jnp.where(row < 20, total * inverse, 0.0)
    rounded = jnp.concatenate([scaled, jnp.zeros((8, 128), F32)], axis=0).astype(BF)
    out[...] = jnp.broadcast_to(rounded[None], out.shape)


def normalize(place, parts):
    return pl.pallas_call(
        normalize_kernel,
        out_shape=jax.ShapeDtypeStruct((16, 32, 128), BF),
        in_specs=[SMEM, VMEM],
        out_specs=VMEM,
        compiler_params=params(),
        name="normalize_tokens",
    )(place, parts)


def moments_kernel(parts, stat):
    for i in range(4):
        q = parts[:, i * 16 : i * 16 + 16, :].reshape(256, 128)
        second = lax.dot_general(q, q, TN, preferred_element_type=F32)
        mean = jnp.sum(q.astype(F32), axis=0, keepdims=True) / QS
        first = jnp.concatenate([mean, jnp.zeros((7, 128), F32)], axis=0)
        outer = lax.dot_general(first, first, TN, preferred_element_type=F32, precision=HIGHEST)
        cov = second / QS - outer
        scaled = mean / math.sqrt(128)
        high = scaled.astype(BF).astype(F32)
        lines = jnp.concatenate([high, scaled - high, jnp.zeros((14, 128), F32)], axis=0)
        stat[0, i, 0:128, :] = cov.astype(BF)
        stat[0, i, 128:144, :] = lines.astype(BF)


def head_moments(parts):
    return pl.pallas_call(
        moments_kernel,
        out_shape=jax.ShapeDtypeStruct((1, 4, STAT, 128), BF),
        in_specs=[VMEM],
        out_specs=VMEM,
        compiler_params=params(),
        name="head_moments",
    )(parts)


def attend_kernel(target, query, bias, send, out, rows, logits, sem):
    items = rows.shape[0]
    width = rows.shape[1]
    wide = width * 4

    def fetch(m):
        return pltpu.make_async_copy(send.at[target[m, 0]], rows.at[m], sem.at[m])

    for m in range(items):
        fetch(m).start()
    head = lax.broadcasted_iota(jnp.int32, (128, wide), 0) // 32
    lane = lax.broadcasted_iota(jnp.int32, (128, wide), 1) % 4
    own = head == lane
    for r in range(2):
        q = query[r * 8 : r * 8 + 8, 0:16, :].reshape(128, 128)
        for b in range(8):
            m = r * 8 + b
            fetch(m).wait()
            keys = rows[m, :, :, 0:128].reshape(wide, 128)
            scores = lax.dot_general(q, keys, NT, preferred_element_type=F32) / math.sqrt(128)
            scores = jnp.where(own, scores, -LARGE) + bias[m : m + 1, :]
            logits[:, b * wide : b * wide + wide] = scores
        top = jnp.max(logits[...], axis=1, keepdims=True)
        total = jnp.zeros((128, 1), F32)
        weighted = jnp.zeros((128, 128), F32)
        for b in range(8):
            weights = jnp.exp(logits[:, b * wide : b * wide + wide] - top)
            total = total + jnp.sum(weights, axis=1, keepdims=True)
            values = rows[r * 8 + b, :, :, 128:256].reshape(wide, 128)
            weighted = weighted + jnp.dot(weights.astype(BF), values, preferred_element_type=F32)
        top_line = jnp.broadcast_to(top, (128, 128)).T[0:1, :]
        total_line = jnp.broadcast_to(total, (128, 128)).T[0:1, :]
        lines = jnp.concatenate([top_line, total_line, jnp.zeros((6, 128), F32)], axis=0)
        for i in range(8):
            out[r * 8 + i, 0:16, :] = weighted[i * 16 : i * 16 + 16, :]
            out[r * 8 + i, 16:24, :] = lines


def attend(target, query, bias, send):
    items, width = send.shape[:2]
    return pl.pallas_call(
        attend_kernel,
        out_shape=jax.ShapeDtypeStruct((16, 24, 128), F32),
        in_specs=[SMEM, VMEM, VMEM, ANY],
        out_specs=VMEM,
        scratch_shapes=[
            pltpu.VMEM(send.shape, send.dtype),
            pltpu.VMEM((128, 8 * width * 4), F32),
            pltpu.SemaphoreType.DMA((items,)),
        ],
        compiler_params=params(16),
        name="attend_kept",
    )(target, query, bias, hbm(send))


def combine_kernel(place, target, parts, query, out, scores):
    p = place[0]
    mine = query[p, 0:16, :]
    pair = (p // 2) * 2
    fresh_key = query[pair, 16:32, :]
    fresh_value = query[pair + 1, 16:32, :]
    recent = lax.dot_general(mine, fresh_key, NT, preferred_element_type=F32) / math.sqrt(128)
    step = lax.broadcasted_iota(jnp.int32, (16, 16), 0) % 4
    column = lax.broadcasted_iota(jnp.int32, (16, 16), 1)
    recent = jnp.where(column <= step, recent, -LARGE)
    row = lax.broadcasted_iota(jnp.int32, (16, 128), 0)
    lane = lax.broadcasted_iota(jnp.int32, (16, 128), 1)
    chosen = lane == (p % 8) * 16 + row
    tops, totals = [], []
    for s in range(16):
        tops.append(jnp.sum(jnp.where(chosen, parts[s, 16:17, :], 0.0), axis=1, keepdims=True))
        totals.append(jnp.sum(jnp.where(chosen, parts[s, 17:18, :], 0.0), axis=1, keepdims=True))
    best = jnp.max(recent, axis=1, keepdims=True)
    for s in range(16):
        best = jnp.maximum(best, tops[s])
    weights = jnp.exp(recent - best)
    total = jnp.sum(weights, axis=1, keepdims=True)
    weighted = jnp.dot(weights.astype(BF), fresh_value, preferred_element_type=F32)
    for s in range(16):
        factor = jnp.exp(tops[s] - best)
        total = total + totals[s] * factor
        weighted = weighted + parts[s, 0:16, :] * factor
    out[...] = jnp.broadcast_to((weighted / total).astype(BF)[None], out.shape)
    for m in range(16):
        start = pl.multiple_of(target[m, 1] * 128, 128)
        scores[m // 8, :, pl.ds(start, 128)] = parts[sender(m, p, target, 16), 18:22, :]


def combine(place, target, parts, query):
    return pl.pallas_call(
        combine_kernel,
        out_shape=(
            jax.ShapeDtypeStruct((16, 16, 128), BF),
            jax.ShapeDtypeStruct((2, 4, 1024), F32),
        ),
        in_specs=[SMEM, SMEM, VMEM, VMEM],
        out_specs=(VMEM, VMEM),
        compiler_params=params(),
        name="combine_parts",
    )(place, target, parts, query)


def reverse_bits(value, order):
    place = 0
    for at, bit in enumerate(order):
        place = place + ((value // bit) % 2) * (1 << at)
    return place


def score_kernel(orders, place, target, stat_a, stat_b, send, parts, out, blocks, sem):
    items = blocks.shape[0]
    lists = items // 2
    me = place[0]

    def fetch(m):
        return pltpu.make_async_copy(send.at[target[m, 0]], blocks.at[m], sem.at[m])

    for m in range(items):
        fetch(m).start()
    out[...] = parts[...]
    for m in range(items):
        fetch(m).wait()
    for r in range(2):
        for j in range(4):
            tables = []
            for o in range(2):
                owner = jnp.bitwise_xor(me, r * 8 + j * 2 + o)
                for half, stat in enumerate((stat_a, stat_b)):
                    tables.append(stat[reverse_bits(owner, orders[half])].reshape(2 * STAT, 128))
            table = jnp.concatenate(tables, axis=0)
            for c in range(lists // 2):
                first = r * lists + c * 2
                keys = blocks[first : first + 2, :, j, 0:128].reshape(256, 128)
                turned_keys = keys.T
                flipped = turned_keys.astype(F32)
                logits = []
                turned = jnp.dot(table, turned_keys, preferred_element_type=F32)
                for g in range(8):
                    base = g * STAT
                    quadratic = jnp.sum(turned[base : base + 128] * flipped, axis=0, keepdims=True)
                    linear = turned[base + 128 : base + 129] + turned[base + 129 : base + 130]
                    logits.append(linear + quadratic / 256.0)
                logit = jnp.concatenate(logits, axis=0)
                top = jnp.max(logit, axis=0, keepdims=True)
                mean = jnp.sum(jnp.exp(logit - top), axis=0, keepdims=True) / 8.0
                line = top + jnp.log(mean)
                for u in range(2):
                    p = target[first + u, 0]
                    out[p, 18 + j : 19 + j, :] = line[:, u * 128 : u * 128 + 128]


def score(orders, place, target, stat_a, stat_b, send, parts):
    items = send.shape[0]

    def kernel(*refs):
        score_kernel(orders, *refs)

    return pl.pallas_call(
        kernel,
        out_shape=jax.ShapeDtypeStruct(parts.shape, parts.dtype),
        in_specs=[SMEM, SMEM, VMEM, VMEM, ANY, VMEM],
        out_specs=VMEM,
        scratch_shapes=[
            pltpu.VMEM(send.shape, send.dtype),
            pltpu.SemaphoreType.DMA((items,)),
        ],
        compiler_params=params(24),
        name="score_kept",
    )(place, target, stat_a, stat_b, hbm(send), parts)


def sender(m, me, target, count):
    return (2 * me - target[m, 0] + count) % count


def place_kernel(place, target, arrived, packed, blocks, in_sem, out_sem):
    items = arrived.shape[0]
    lists = items // 2

    def fetch(m):
        return pltpu.make_async_copy(
            arrived.at[sender(m, place[0], target, items)], blocks.at[m], in_sem.at[m]
        )

    def put(m):
        slot = (m // lists) * lists + target[m, 1]
        return pltpu.make_async_copy(blocks.at[m], packed.at[slot], out_sem.at[m])

    for m in range(items):
        fetch(m).start()
    for m in range(items):
        fetch(m).wait()
        put(m).start()
    for m in range(items):
        put(m).wait()


def put_blocks(place, target, arrived):
    items = arrived.shape[0]
    return pl.pallas_call(
        place_kernel,
        out_shape=pltpu.HBM(arrived.shape, arrived.dtype),
        in_specs=[SMEM, SMEM, ANY],
        out_specs=ANY,
        scratch_shapes=[
            pltpu.VMEM(arrived.shape, arrived.dtype),
            pltpu.SemaphoreType.DMA((items,)),
            pltpu.SemaphoreType.DMA((items,)),
        ],
        compiler_params=params(),
        name="place_blocks",
    )(place, target, hbm(arrived))


def finish_kernel(joined, w, out, rows, weight, sem):
    quarter = w.shape[0] // 4

    def fetch(i):
        part = pl.ds(i * quarter, quarter)
        return pltpu.make_async_copy(w.at[part], weight.at[part], sem.at[i])

    for i in range(4):
        fetch(i).start()
    for r in range(2):
        for h in range(32):
            at = (h % 4) * 4
            rows[r * 4 : r * 4 + 4, h * 128 : h * 128 + 128] = joined[
                r * 8 + h // 4, at : at + 4, :
            ].astype(F32)
    value = jnp.zeros((8, w.shape[1]), F32)
    for i in range(4):
        fetch(i).wait()
        part = slice(i * quarter, i * quarter + quarter)
        value = value + jnp.dot(
            rows[:, part].astype(BF), weight[part, :], preferred_element_type=F32
        )
    for r in range(2):
        for t in range(4):
            out[t, r : r + 1, :] = value[r * 4 + t : r * 4 + t + 1, :]


def finish(joined, w_out):
    return pl.pallas_call(
        finish_kernel,
        out_shape=jax.ShapeDtypeStruct((4, 2, w_out.shape[1]), F32),
        in_specs=[VMEM, ANY],
        out_specs=VMEM,
        scratch_shapes=[
            pltpu.VMEM((8, w_out.shape[0]), F32),
            pltpu.VMEM(w_out.shape, w_out.dtype),
            pltpu.SemaphoreType.DMA((4,)),
        ],
        compiler_params=params(),
        name="project_out",
    )(joined, hbm(w_out))


def exchange(value):
    return lax.all_to_all(value, "ctx", split_axis=0, concat_axis=0, tiled=True)


def doubled(value, bit):
    pairs = [(i, i ^ bit) for i in range(16)]
    return jnp.concatenate([value, lax.ppermute(value, "ctx", pairs)], axis=0)


def after(values, token):
    return lax.optimization_barrier((values, token))[0]


ORDERS = ((8, 4, 2, 1), (8, 4, 1, 2))


def sixteen(
    kv_cache, keep_rows, block_target, future_queries, new_tokens, w_query, w_keyval, w_out
):
    requests, cache_rows, local_kv, pair = kv_cache.shape
    lists, width = keep_rows.shape[1:]
    items = requests * lists
    keep = keep_rows.reshape(items, width)
    target = block_target.reshape(items, 2)
    place = lax.axis_index("ctx").astype(jnp.int32).reshape(1)
    samples = exchange(split_samples(future_queries))
    parts, samples = lax.optimization_barrier((project(new_tokens, w_query, w_keyval), samples))
    parts = exchange(parts)
    stat = doubled(head_moments(samples), 8)
    send = pack(kv_cache, after(keep, samples), target)
    stat = doubled(after(stat, send), 4)
    query = exchange(normalize(place, after(parts, send)))
    arrived = exchange(after(send, (query, stat)))
    bias = jnp.where(after(keep, query) < 2 * width, 0.0, -LARGE).astype(F32)
    bias = jnp.broadcast_to(bias[:, :, None], (items, width, 4)).reshape(items, width * 4)
    stat_a = doubled(doubled(stat[:, :2], 2), 1)
    stat_b = doubled(doubled(stat[:, 2:], 1), 2)
    softmax = attend(target, query, bias, send)
    softmax = score(ORDERS, place, target, stat_a, stat_b, send, softmax)
    parts = exchange(after(softmax, arrived))
    packed = put_blocks(place, target, arrived)
    share, scores = combine(place, target, after(parts, packed), query)
    attended = exchange(share)
    decoded = lax.psum(finish(attended, w_out), "head").astype(BF)
    return packed.reshape(requests, lists * width, local_kv, pair), scores, decoded


def joined(value, axis, join):
    pieces = jax.tree.map(lambda part: lax.all_gather(part, axis), value)
    head = jax.tree.map(lambda part: part[0], pieces)
    tail = jax.tree.map(lambda part: part[1:], pieces)
    running, _ = lax.scan(lambda running, share: (join(running, share), None), head, tail)
    return running


def group_scores(keys, mean_q, cov_q):
    lifted = keys.astype(jnp.float32)
    linear = jnp.einsum("nkd,kgd->nkg", lifted, mean_q, precision=HIGHEST)
    turned = jnp.einsum("nkd,kgde->nkge", lifted, cov_q, precision=HIGHEST)
    quadratic = jnp.sum(turned * lifted[:, :, None, :], axis=-1)
    logits = linear / math.sqrt(keys.shape[-1]) + quadratic / (2.0 * keys.shape[-1])
    top = jnp.max(logits, axis=2)
    return top + jnp.log(jnp.mean(jnp.exp(logits - top[:, :, None]), axis=2))


def combine_parts(first, second):
    top_a, total_a, weighted_a = first
    top_b, total_b, weighted_b = second
    best = jnp.maximum(top_a, top_b)
    factor_a = jnp.exp(top_a - best)
    factor_b = jnp.exp(top_b - best)
    return (
        best,
        total_a * factor_a + total_b * factor_b,
        weighted_a * factor_a[..., None] + weighted_b * factor_b[..., None],
    )


def moments(sample):
    second = jnp.einsum("rshd,rshe->rhde", sample, sample, preferred_element_type=jnp.float32)
    summed = jnp.sum(sample.astype(jnp.float32), axis=1)
    return (second, summed)


KVH = 8


def per_device(
    kv_cache, keep_rows, block_target, future_queries, new_tokens, w_query, w_keyval, w_out
):
    requests, cache_rows, local_kv, pair = kv_cache.shape
    head_size = pair // 2
    lists, width = (keep_rows.shape[1], keep_rows.shape[2])
    span = 2 * width
    group = H // KVH
    ctx_count = lax.axis_size("ctx")
    position = lax.axis_index("ctx")
    root_size = math.sqrt(head_size)
    sample = future_queries.reshape(requests, -1, local_kv * group, head_size)
    second, summed = moments(sample)
    second, summed = lax.psum((second, summed), "ctx")
    mean_q = summed / QS
    cov_q = second / QS - mean_q[..., :, None] * mean_q[..., None, :]
    mean_q = mean_q.reshape(requests, local_kv, group, head_size)
    cov_q = cov_q.reshape(requests, local_kv, group, head_size, head_size)
    span_index = jnp.arange(span, dtype=jnp.int32)
    block_kv, block_score, block_count = ([], [], [])
    for request in range(requests):
        listed = keep_rows[request]
        picker = (listed[:, :, None] == span_index[None, None, :]).astype(jnp.bfloat16)
        spans = kv_cache[request].reshape(lists, span, local_kv * pair)
        chosen = jnp.einsum(
            "bjs,bsc->bjc", picker, spans, preferred_element_type=jnp.float32
        ).astype(jnp.bfloat16)
        chosen = chosen.reshape(lists, width, local_kv, pair)
        every = group_scores(kv_cache[request][:, :, :head_size], mean_q[request], cov_q[request])
        every = every.reshape(lists, span, local_kv)
        picked = jnp.einsum("bjs,bsk->bkj", picker.astype(jnp.float32), every, precision=HIGHEST)
        block_kv.append(chosen)
        block_score.append(picked)
        block_count.append(jnp.sum((listed < span).astype(jnp.int32), axis=1))
    items_kv = jnp.concatenate(block_kv, axis=0)
    items_score = jnp.concatenate(block_score, axis=0)
    items_count = jnp.concatenate(block_count, axis=0)
    total_items = requests * lists
    targets = block_target.reshape(total_items, 2)
    offset = (targets[:, 0] - position) % ctx_count
    slot = targets[:, 1].reshape(requests, lists)
    peers = jnp.arange(ctx_count, dtype=jnp.int32)
    outgoing = targets[:, 0][None, :] == peers[:, None]
    send_kv = jnp.einsum(
        "pm,mjkc->pjkc", outgoing.astype(jnp.bfloat16), items_kv, preferred_element_type=jnp.float32
    ).astype(jnp.bfloat16)
    send_score = jnp.einsum(
        "pm,mkj->pkj", outgoing.astype(jnp.float32), items_score, precision=HIGHEST
    )
    send_count = jnp.sum(jnp.where(outgoing, items_count[None, :], 0), axis=1)
    recv_kv, recv_score, recv_count = (
        lax.all_to_all(send_kv, "ctx", split_axis=0, concat_axis=0, tiled=True),
        lax.all_to_all(
            send_score.astype(jnp.bfloat16), "ctx", split_axis=0, concat_axis=0, tiled=True
        ).astype(send_score.dtype),
        lax.all_to_all(send_count, "ctx", split_axis=0, concat_axis=0, tiled=True),
    )
    source = (position - offset) % ctx_count
    incoming = source[:, None] == peers[None, :]
    got_kv = jnp.einsum(
        "mp,pjkc->mjkc", incoming.astype(jnp.bfloat16), recv_kv, preferred_element_type=jnp.float32
    ).astype(jnp.bfloat16)
    got_score = jnp.einsum(
        "mp,pkj->mkj", incoming.astype(jnp.float32), recv_score, precision=HIGHEST
    )
    got_count = jnp.sum(jnp.where(incoming, recv_count[None, :], 0), axis=1)
    slot_table = slot[:, None, :] == jnp.arange(lists, dtype=jnp.int32)[None, :, None]
    placed_kv = jnp.einsum(
        "rsb,rbjkc->rsjkc",
        slot_table.astype(jnp.bfloat16),
        got_kv.reshape(requests, lists, width, local_kv, pair),
        preferred_element_type=jnp.float32,
    ).astype(jnp.bfloat16)
    packed_cache = placed_kv.reshape(requests, lists * width, local_kv, pair)
    placed_score = jnp.einsum(
        "rsb,rbkj->rksj",
        slot_table.astype(jnp.float32),
        got_score.reshape(requests, lists, local_kv, width),
        precision=HIGHEST,
    )
    packed_scores = placed_score.reshape(requests, local_kv, lists * width)
    placed_count = jnp.sum(jnp.where(slot_table, got_count.reshape(requests, 1, lists), 0), axis=2)
    live = (jnp.arange(width, dtype=jnp.int32)[None, None, :] < placed_count[:, :, None]).reshape(
        requests, lists * width
    )
    steps = new_tokens.shape[0]
    local_width = new_tokens.shape[2]
    flat = new_tokens.reshape(steps * requests, local_width)
    wide = flat.astype(jnp.float32)
    squares = jnp.sum(wide * wide, axis=1)
    query_part = jnp.dot(flat, w_query, preferred_element_type=jnp.float32)
    pair_part = jnp.dot(
        flat, w_keyval.reshape(local_width, local_kv * pair), preferred_element_type=jnp.float32
    )
    squares, query_part, pair_part = lax.psum((squares, query_part, pair_part), "ctx")
    inverse = lax.rsqrt(squares / D + EPSILON)
    query = (
        (query_part * inverse[:, None])
        .astype(jnp.bfloat16)
        .reshape(steps, requests, local_kv, group, head_size)
    )
    fresh = (
        (pair_part * inverse[:, None]).astype(jnp.bfloat16).reshape(steps, requests, local_kv, pair)
    )
    query = jnp.transpose(query, (1, 2, 0, 3, 4)).reshape(
        requests, local_kv, steps * group, head_size
    )
    fresh = jnp.transpose(fresh, (1, 2, 0, 3))
    logits = (
        jnp.einsum(
            "rkqd,rnkd->rkqn",
            query,
            packed_cache[..., :head_size],
            preferred_element_type=jnp.float32,
        )
        / root_size
    )
    logits = jnp.where(live[:, None, None, :], logits, -jnp.inf)
    top = jnp.max(logits, axis=3)
    weights = jnp.exp(logits - top[..., None])
    totals = jnp.sum(weights, axis=3)
    weighted = jnp.einsum(
        "rkqn,rnkd->rkqd",
        weights.astype(jnp.bfloat16),
        packed_cache[..., head_size:],
        preferred_element_type=jnp.float32,
    )
    top, totals, weighted = joined((top, totals, weighted), "ctx", combine_parts)
    recent = (
        jnp.einsum(
            "rkqd,rkud->rkqu", query, fresh[..., :head_size], preferred_element_type=jnp.float32
        )
        / root_size
    )
    causal = (jnp.arange(steps * group, dtype=jnp.int32) // group)[:, None] >= jnp.arange(
        steps, dtype=jnp.int32
    )[None, :]
    recent = jnp.where(causal[None, None], recent, -jnp.inf)
    best = jnp.maximum(top, jnp.max(recent, axis=3))
    weight_new = jnp.exp(recent - best[..., None])
    factor_old = jnp.exp(top - best)
    normalizer = totals * factor_old + jnp.sum(weight_new, axis=3)
    weighted = weighted * factor_old[..., None] + jnp.einsum(
        "rkqu,rkud->rkqd",
        weight_new.astype(jnp.bfloat16),
        fresh[..., head_size:],
        preferred_element_type=jnp.float32,
    )
    attended = (weighted / normalizer[..., None]).astype(jnp.bfloat16)
    attended = attended.reshape(requests, local_kv, steps, group, head_size)
    attended = jnp.transpose(attended, (2, 0, 1, 3, 4)).reshape(
        steps * requests, local_kv * group * head_size
    )
    partial_value = jnp.dot(attended, w_out, preferred_element_type=jnp.float32)
    summed_out = lax.psum(partial_value, "head")
    decoded = summed_out.astype(jnp.bfloat16).reshape(steps, requests, local_width)
    return (packed_cache, packed_scores, decoded)


def solution(mesh):
    in_specs = (
        P(None, "ctx", "head", None),
        P(None, "ctx", None),
        P(None, "ctx", None),
        P(None, "ctx", "head"),
        P(None, None, "ctx"),
        P("ctx", "head"),
        P("ctx", "head", None),
        P("head", "ctx"),
    )
    out_specs = (P(None, "ctx", "head", None), P(None, "head", "ctx"), P(None, None, "ctx"))
    body = sixteen if mesh.shape["ctx"] == 16 and mesh.shape["head"] == 2 else per_device
    return jax.shard_map(
        body, mesh=mesh, in_specs=in_specs, out_specs=out_specs, check_vma=False
    )
```

```python
import math

import jax
import jax.numpy as jnp
from jax import lax
from jax.experimental import pallas as pl
from jax.experimental.pallas import tpu as pltpu
from jax.sharding import PartitionSpec as P

D = 8192
H = 64
QS = 256
EPSILON = 1e-05
HIGHEST = lax.Precision.HIGHEST
BF = jnp.bfloat16
F32 = jnp.float32
STAT = 144
LARGE = 1e30
ANY = pl.BlockSpec(memory_space=pltpu.HBM)
SMEM = pl.BlockSpec(memory_space=pltpu.SMEM)
VMEM = pl.BlockSpec(memory_space=pltpu.VMEM)
NT = (((1,), (1,)), ((), ()))
TN = (((0,), (0,)), ((), ()))


def hbm(value):
    return pltpu.with_memory_space_constraint(value, pltpu.HBM)


def params(megabytes=8):
    return pltpu.CompilerParams(vmem_limit_bytes=megabytes << 20)


def pack_kernel(keep, target, kv, send, spans, blocks, in_sem, out_sem):
    items, width = keep.shape
    span = 2 * width
    lists = items // kv.shape[0]

    def fetch(m):
        return pltpu.make_async_copy(
            kv.at[m // lists, pl.ds((m % lists) * span, span)], spans.at[m, pl.ds(0, span)], in_sem.at[m]
        )

    def put(m):
        return pltpu.make_async_copy(blocks.at[m], send.at[target[m, 0]], out_sem.at[m])

    for m in range(items):
        fetch(m).start()
        spans[m, span] = jnp.zeros(spans.shape[2:], spans.dtype)

    for m in range(items):
        fetch(m).wait()

        def rows(j, inner):
            values = [spans[m, keep[m, j * 32 + u]] for u in range(32)]
            for u in range(32):
                blocks[m, j * 32 + u] = values[u]
            return inner

        lax.fori_loop(0, width // 32, rows, 0)
        put(m).start()
    for m in range(items):
        put(m).wait()


def pack(kv_cache, keep, target):
    items, width = keep.shape
    tail = kv_cache.shape[2:]
    return pl.pallas_call(
        pack_kernel,
        out_shape=pltpu.HBM((items, width, *tail), kv_cache.dtype),
        in_specs=[SMEM, SMEM, ANY],
        out_specs=ANY,
        scratch_shapes=[
            pltpu.VMEM((items, 2 * width + 8, *tail), kv_cache.dtype),
            pltpu.VMEM((items, width, *tail), kv_cache.dtype),
            pltpu.SemaphoreType.DMA((items,)),
            pltpu.SemaphoreType.DMA((items,)),
        ],
        compiler_params=params(20),
        name="pack_rows",
    )(keep, target, hbm(kv_cache))


def split_kernel(samples, out):
    for r in range(2):
        for c in range(32):
            out[r * 8 + c // 4, (c % 4) * 16 : (c % 4) * 16 + 16, :] = samples[
                r, :, c * 128 : c * 128 + 128
            ]


def split_samples(samples):
    return pl.pallas_call(
        split_kernel,
        out_shape=jax.ShapeDtypeStruct((16, 64, 128), BF),
        in_specs=[VMEM],
        out_specs=VMEM,
        compiler_params=params(),
        name="split_samples",
    )(samples)


def project_kernel(tokens, wq, wkv, out):
    i = pl.program_id(0)
    x = jnp.concatenate([tokens[t, r : r + 1, :].astype(F32) for r in range(2) for t in range(4)], axis=0)
    x = x.astype(BF)
    part = jnp.dot(x, wq[...], preferred_element_type=F32)
    for r in range(2):
        for g in range(8):
            out[r * 8 + i * 2 + g // 4, (g % 4) * 4 : (g % 4) * 4 + 4, :] = part[
                r * 4 : r * 4 + 4, g * 128 : g * 128 + 128
            ]

    @pl.when(i == 0)
    def _():
        heads = pltpu.einshape("nhd->hnd", wkv[...])
        wide = x.astype(F32)
        squares = jnp.sum(wide * wide, axis=1, keepdims=True)
        row = lax.broadcasted_iota(jnp.int32, (8, 128), 0)
        lane = lax.broadcasted_iota(jnp.int32, (8, 128), 1)
        line = jnp.sum(jnp.where(row == lane, squares, 0.0), axis=0, keepdims=True)
        line = jnp.concatenate([line, jnp.zeros((3, 128), F32)], axis=0)
        for p in range(16):
            out[p, 20:24, :] = line
        for j in range(4):
            pair = jnp.dot(x, heads[j], preferred_element_type=F32)
            for r in range(2):
                for half in range(2):
                    out[r * 8 + j * 2 + half, 16:20, :] = pair[
                        r * 4 : r * 4 + 4, half * 128 : half * 128 + 128
                    ]


def project(tokens, w_query, w_keyval):
    depth, columns = w_query.shape
    step = columns // 4
    return pl.pallas_call(
        project_kernel,
        out_shape=jax.ShapeDtypeStruct((16, 24, 128), F32),
        grid=(4,),
        in_specs=[
            pl.BlockSpec(tokens.shape, lambda i: (0, 0, 0)),
            pl.BlockSpec((depth, step), lambda i: (0, i)),
            pl.BlockSpec(w_keyval.shape, lambda i: (0, 0, 0)),
        ],
        out_specs=pl.BlockSpec((16, 24, 128), lambda i: (0, 0, 0)),
        compiler_params=params(16),
        name="project_tokens",
    )(hbm(tokens), hbm(w_query), hbm(w_keyval))


def normalize_kernel(place, parts, out):
    total = jnp.sum(parts[...], axis=0)
    request = place[0] // 8
    row = lax.broadcasted_iota(jnp.int32, (24, 128), 0)
    lane = lax.broadcasted_iota(jnp.int32, (24, 128), 1)
    squares = jnp.where(lane == request * 4 + row % 4, total[20:21, :], 0.0)
    inverse = lax.rsqrt(jnp.sum(squares, axis=1, keepdims=True) / D + EPSILON)
    scaled = jnp.where(row < 20, total * inverse, 0.0)
    rounded = jnp.concatenate([scaled, jnp.zeros((8, 128), F32)], axis=0).astype(BF)
    out[...] = jnp.broadcast_to(rounded[None], out.shape)


def normalize(place, parts):
    return pl.pallas_call(
        normalize_kernel,
        out_shape=jax.ShapeDtypeStruct((16, 32, 128), BF),
        in_specs=[SMEM, VMEM],
        out_specs=VMEM,
        compiler_params=params(),
        name="normalize_tokens",
    )(place, parts)


def moments_kernel(parts, stat):
    for i in range(4):
        q = parts[:, i * 16 : i * 16 + 16, :].reshape(256, 128)
        second = lax.dot_general(q, q, TN, preferred_element_type=F32)
        mean = jnp.sum(q.astype(F32), axis=0, keepdims=True) / QS
        first = jnp.concatenate([mean, jnp.zeros((7, 128), F32)], axis=0)
        outer = lax.dot_general(first, first, TN, preferred_element_type=F32, precision=HIGHEST)
        cov = second / QS - outer
        scaled = mean / math.sqrt(128)
        high = scaled.astype(BF).astype(F32)
        lines = jnp.concatenate([high, scaled - high, jnp.zeros((14, 128), F32)], axis=0)
        stat[0, i, 0:128, :] = cov.astype(BF)
        stat[0, i, 128:144, :] = lines.astype(BF)


def head_moments(parts):
    return pl.pallas_call(
        moments_kernel,
        out_shape=jax.ShapeDtypeStruct((1, 4, STAT, 128), BF),
        in_specs=[VMEM],
        out_specs=VMEM,
        compiler_params=params(),
        name="head_moments",
    )(parts)


def attend_kernel(target, query, bias, send, out, rows, logits, sem):
    items = rows.shape[0]
    width = rows.shape[1]
    wide = width * 4

    def fetch(m):
        return pltpu.make_async_copy(send.at[target[m, 0]], rows.at[m], sem.at[m])

    for m in range(items):
        fetch(m).start()
    head = lax.broadcasted_iota(jnp.int32, (128, wide), 0) // 32
    lane = lax.broadcasted_iota(jnp.int32, (128, wide), 1) % 4
    own = head == lane
    for r in range(2):
        q = query[r * 8 : r * 8 + 8, 0:16, :].reshape(128, 128)
        for b in range(8):
            m = r * 8 + b
            fetch(m).wait()
            keys = rows[m, :, :, 0:128].reshape(wide, 128)
            scores = lax.dot_general(q, keys, NT, preferred_element_type=F32) / math.sqrt(128)
            scores = jnp.where(own, scores, -LARGE) + bias[m : m + 1, :]
            logits[:, b * wide : b * wide + wide] = scores
        top = jnp.max(logits[...], axis=1, keepdims=True)
        total = jnp.zeros((128, 1), F32)
        weighted = jnp.zeros((128, 128), F32)
        for b in range(8):
            weights = jnp.exp(logits[:, b * wide : b * wide + wide] - top)
            total = total + jnp.sum(weights, axis=1, keepdims=True)
            values = rows[r * 8 + b, :, :, 128:256].reshape(wide, 128)
            weighted = weighted + jnp.dot(weights.astype(BF), values, preferred_element_type=F32)
        top_line = jnp.broadcast_to(top, (128, 128)).T[0:1, :]
        total_line = jnp.broadcast_to(total, (128, 128)).T[0:1, :]
        lines = jnp.concatenate([top_line, total_line, jnp.zeros((6, 128), F32)], axis=0)
        for i in range(8):
            out[r * 8 + i, 0:16, :] = weighted[i * 16 : i * 16 + 16, :]
            out[r * 8 + i, 16:24, :] = lines


def attend(target, query, bias, send):
    items, width = send.shape[:2]
    return pl.pallas_call(
        attend_kernel,
        out_shape=jax.ShapeDtypeStruct((16, 24, 128), F32),
        in_specs=[SMEM, VMEM, VMEM, ANY],
        out_specs=VMEM,
        scratch_shapes=[
            pltpu.VMEM(send.shape, send.dtype),
            pltpu.VMEM((128, 8 * width * 4), F32),
            pltpu.SemaphoreType.DMA((items,)),
        ],
        compiler_params=params(16),
        name="attend_kept",
    )(target, query, bias, hbm(send))


def combine_kernel(place, target, parts, query, out, scores):
    p = place[0]
    mine = query[p, 0:16, :]
    pair = (p // 2) * 2
    fresh_key = query[pair, 16:32, :]
    fresh_value = query[pair + 1, 16:32, :]
    recent = lax.dot_general(mine, fresh_key, NT, preferred_element_type=F32) / math.sqrt(128)
    step = lax.broadcasted_iota(jnp.int32, (16, 16), 0) % 4
    column = lax.broadcasted_iota(jnp.int32, (16, 16), 1)
    recent = jnp.where(column <= step, recent, -LARGE)
    row = lax.broadcasted_iota(jnp.int32, (16, 128), 0)
    lane = lax.broadcasted_iota(jnp.int32, (16, 128), 1)
    chosen = lane == (p % 8) * 16 + row
    tops, totals = [], []
    for s in range(16):
        tops.append(jnp.sum(jnp.where(chosen, parts[s, 16:17, :], 0.0), axis=1, keepdims=True))
        totals.append(jnp.sum(jnp.where(chosen, parts[s, 17:18, :], 0.0), axis=1, keepdims=True))
    best = jnp.max(recent, axis=1, keepdims=True)
    for s in range(16):
        best = jnp.maximum(best, tops[s])
    weights = jnp.exp(recent - best)
    total = jnp.sum(weights, axis=1, keepdims=True)
    weighted = jnp.dot(weights.astype(BF), fresh_value, preferred_element_type=F32)
    for s in range(16):
        factor = jnp.exp(tops[s] - best)
        total = total + totals[s] * factor
        weighted = weighted + parts[s, 0:16, :] * factor
    out[...] = jnp.broadcast_to((weighted / total).astype(BF)[None], out.shape)
    for m in range(16):
        start = pl.multiple_of(target[m, 1] * 128, 128)
        scores[m // 8, :, pl.ds(start, 128)] = parts[sender(m, p, target, 16), 18:22, :]


def combine(place, target, parts, query):
    return pl.pallas_call(
        combine_kernel,
        out_shape=(
            jax.ShapeDtypeStruct((16, 16, 128), BF),
            jax.ShapeDtypeStruct((2, 4, 1024), F32),
        ),
        in_specs=[SMEM, SMEM, VMEM, VMEM],
        out_specs=(VMEM, VMEM),
        compiler_params=params(),
        name="combine_parts",
    )(place, target, parts, query)


def reverse_bits(value, order):
    place = 0
    for at, bit in enumerate(order):
        place = place + ((value // bit) % 2) * (1 << at)
    return place


def score_kernel(orders, place, target, stat_a, stat_b, send, parts, out, blocks, sem):
    items = blocks.shape[0]
    lists = items // 2
    me = place[0]

    def fetch(m):
        return pltpu.make_async_copy(send.at[target[m, 0]], blocks.at[m], sem.at[m])

    for m in range(items):
        fetch(m).start()
    out[...] = parts[...]
    for m in range(items):
        fetch(m).wait()
    for r in range(2):
        for j in range(4):
            tables = []
            for o in range(2):
                owner = jnp.bitwise_xor(me, r * 8 + j * 2 + o)
                for half, stat in enumerate((stat_a, stat_b)):
                    tables.append(stat[reverse_bits(owner, orders[half])].reshape(2 * STAT, 128))
            table = jnp.concatenate(tables, axis=0)
            for c in range(lists // 2):
                first = r * lists + c * 2
                keys = blocks[first : first + 2, :, j, 0:128].reshape(256, 128)
                turned_keys = keys.T
                flipped = turned_keys.astype(F32)
                logits = []
                turned = jnp.dot(table, turned_keys, preferred_element_type=F32)
                for g in range(8):
                    base = g * STAT
                    quadratic = jnp.sum(turned[base : base + 128] * flipped, axis=0, keepdims=True)
                    linear = turned[base + 128 : base + 129] + turned[base + 129 : base + 130]
                    logits.append(linear + quadratic / 256.0)
                logit = jnp.concatenate(logits, axis=0)
                top = jnp.max(logit, axis=0, keepdims=True)
                mean = jnp.sum(jnp.exp(logit - top), axis=0, keepdims=True) / 8.0
                line = top + jnp.log(mean)
                for u in range(2):
                    p = target[first + u, 0]
                    out[p, 18 + j : 19 + j, :] = line[:, u * 128 : u * 128 + 128]


def score(orders, place, target, stat_a, stat_b, send, parts):
    items = send.shape[0]

    def kernel(*refs):
        score_kernel(orders, *refs)

    return pl.pallas_call(
        kernel,
        out_shape=jax.ShapeDtypeStruct(parts.shape, parts.dtype),
        in_specs=[SMEM, SMEM, VMEM, VMEM, ANY, VMEM],
        out_specs=VMEM,
        scratch_shapes=[
            pltpu.VMEM(send.shape, send.dtype),
            pltpu.SemaphoreType.DMA((items,)),
        ],
        compiler_params=params(24),
        name="score_kept",
    )(place, target, stat_a, stat_b, hbm(send), parts)


def sender(m, me, target, count):
    return (2 * me - target[m, 0] + count) % count


def place_kernel(place, target, arrived, packed, blocks, in_sem, out_sem):
    items = arrived.shape[0]
    lists = items // 2

    def fetch(m):
        return pltpu.make_async_copy(
            arrived.at[sender(m, place[0], target, items)], blocks.at[m], in_sem.at[m]
        )

    def put(m):
        slot = (m // lists) * lists + target[m, 1]
        return pltpu.make_async_copy(blocks.at[m], packed.at[slot], out_sem.at[m])

    for m in range(items):
        fetch(m).start()
    for m in range(items):
        fetch(m).wait()
        put(m).start()
    for m in range(items):
        put(m).wait()


def put_blocks(place, target, arrived):
    items = arrived.shape[0]
    return pl.pallas_call(
        place_kernel,
        out_shape=pltpu.HBM(arrived.shape, arrived.dtype),
        in_specs=[SMEM, SMEM, ANY],
        out_specs=ANY,
        scratch_shapes=[
            pltpu.VMEM(arrived.shape, arrived.dtype),
            pltpu.SemaphoreType.DMA((items,)),
            pltpu.SemaphoreType.DMA((items,)),
        ],
        compiler_params=params(),
        name="place_blocks",
    )(place, target, hbm(arrived))


def finish_kernel(joined, w, out, rows, weight, sem):
    quarter = w.shape[0] // 4

    def fetch(i):
        part = pl.ds(i * quarter, quarter)
        return pltpu.make_async_copy(w.at[part], weight.at[part], sem.at[i])

    for i in range(4):
        fetch(i).start()
    for r in range(2):
        for h in range(32):
            at = (h % 4) * 4
            rows[r * 4 : r * 4 + 4, h * 128 : h * 128 + 128] = joined[
                r * 8 + h // 4, at : at + 4, :
            ].astype(F32)
    value = jnp.zeros((8, w.shape[1]), F32)
    for i in range(4):
        fetch(i).wait()
        part = slice(i * quarter, i * quarter + quarter)
        value = value + jnp.dot(
            rows[:, part].astype(BF), weight[part, :], preferred_element_type=F32
        )
    for r in range(2):
        for t in range(4):
            out[t, r : r + 1, :] = value[r * 4 + t : r * 4 + t + 1, :]


def finish(joined, w_out):
    return pl.pallas_call(
        finish_kernel,
        out_shape=jax.ShapeDtypeStruct((4, 2, w_out.shape[1]), F32),
        in_specs=[VMEM, ANY],
        out_specs=VMEM,
        scratch_shapes=[
            pltpu.VMEM((8, w_out.shape[0]), F32),
            pltpu.VMEM(w_out.shape, w_out.dtype),
            pltpu.SemaphoreType.DMA((4,)),
        ],
        compiler_params=params(),
        name="project_out",
    )(joined, hbm(w_out))


def exchange(value):
    return lax.all_to_all(value, "ctx", split_axis=0, concat_axis=0, tiled=True)


def doubled(value, bit):
    pairs = [(i, i ^ bit) for i in range(16)]
    return jnp.concatenate([value, lax.ppermute(value, "ctx", pairs)], axis=0)


def after(values, token):
    return lax.optimization_barrier((values, token))[0]


ORDERS = ((8, 4, 2, 1), (8, 4, 1, 2))


def sixteen(
    kv_cache, keep_rows, block_target, future_queries, new_tokens, w_query, w_keyval, w_out
):
    requests, cache_rows, local_kv, pair = kv_cache.shape
    lists, width = keep_rows.shape[1:]
    items = requests * lists
    keep = keep_rows.reshape(items, width)
    target = block_target.reshape(items, 2)
    place = lax.axis_index("ctx").astype(jnp.int32).reshape(1)
    samples = exchange(split_samples(future_queries))
    parts, samples = lax.optimization_barrier((project(new_tokens, w_query, w_keyval), samples))
    parts = exchange(parts)
    stat = doubled(head_moments(samples), 8)
    send = pack(kv_cache, after(keep, samples), target)
    stat = doubled(after(stat, send), 4)
    query = exchange(normalize(place, after(parts, send)))
    arrived = exchange(after(send, (query, stat)))
    bias = jnp.where(after(keep, query) < 2 * width, 0.0, -LARGE).astype(F32)
    bias = jnp.broadcast_to(bias[:, :, None], (items, width, 4)).reshape(items, width * 4)
    stat_a = doubled(doubled(stat[:, :2], 2), 1)
    stat_b = doubled(doubled(stat[:, 2:], 1), 2)
    softmax = attend(target, query, bias, send)
    softmax = score(ORDERS, place, target, stat_a, stat_b, send, softmax)
    parts = exchange(after(softmax, arrived))
    packed = put_blocks(place, target, arrived)
    share, scores = combine(place, target, after(parts, packed), query)
    attended = exchange(share)
    decoded = lax.psum(finish(attended, w_out), "head").astype(BF)
    return packed.reshape(requests, lists * width, local_kv, pair), scores, decoded


def joined(value, axis, join):
    pieces = jax.tree.map(lambda part: lax.all_gather(part, axis), value)
    head = jax.tree.map(lambda part: part[0], pieces)
    tail = jax.tree.map(lambda part: part[1:], pieces)
    running, _ = lax.scan(lambda running, share: (join(running, share), None), head, tail)
    return running


def group_scores(keys, mean_q, cov_q):
    lifted = keys.astype(jnp.float32)
    linear = jnp.einsum("nkd,kgd->nkg", lifted, mean_q, precision=HIGHEST)
    turned = jnp.einsum("nkd,kgde->nkge", lifted, cov_q, precision=HIGHEST)
    quadratic = jnp.sum(turned * lifted[:, :, None, :], axis=-1)
    logits = linear / math.sqrt(keys.shape[-1]) + quadratic / (2.0 * keys.shape[-1])
    top = jnp.max(logits, axis=2)
    return top + jnp.log(jnp.mean(jnp.exp(logits - top[:, :, None]), axis=2))


def combine_parts(first, second):
    top_a, total_a, weighted_a = first
    top_b, total_b, weighted_b = second
    best = jnp.maximum(top_a, top_b)
    factor_a = jnp.exp(top_a - best)
    factor_b = jnp.exp(top_b - best)
    return (
        best,
        total_a * factor_a + total_b * factor_b,
        weighted_a * factor_a[..., None] + weighted_b * factor_b[..., None],
    )


def moments(sample):
    second = jnp.einsum("rshd,rshe->rhde", sample, sample, preferred_element_type=jnp.float32)
    summed = jnp.sum(sample.astype(jnp.float32), axis=1)
    return (second, summed)


KVH = 8


def per_device(
    kv_cache, keep_rows, block_target, future_queries, new_tokens, w_query, w_keyval, w_out
):
    requests, cache_rows, local_kv, pair = kv_cache.shape
    head_size = pair // 2
    lists, width = (keep_rows.shape[1], keep_rows.shape[2])
    span = 2 * width
    group = H // KVH
    ctx_count = lax.axis_size("ctx")
    position = lax.axis_index("ctx")
    root_size = math.sqrt(head_size)
    sample = future_queries.reshape(requests, -1, local_kv * group, head_size)
    second, summed = moments(sample)
    second, summed = lax.psum((second, summed), "ctx")
    mean_q = summed / QS
    cov_q = second / QS - mean_q[..., :, None] * mean_q[..., None, :]
    mean_q = mean_q.reshape(requests, local_kv, group, head_size)
    cov_q = cov_q.reshape(requests, local_kv, group, head_size, head_size)
    span_index = jnp.arange(span, dtype=jnp.int32)
    block_kv, block_score, block_count = ([], [], [])
    for request in range(requests):
        listed = keep_rows[request]
        picker = (listed[:, :, None] == span_index[None, None, :]).astype(jnp.bfloat16)
        spans = kv_cache[request].reshape(lists, span, local_kv * pair)
        chosen = jnp.einsum(
            "bjs,bsc->bjc", picker, spans, preferred_element_type=jnp.float32
        ).astype(jnp.bfloat16)
        chosen = chosen.reshape(lists, width, local_kv, pair)
        every = group_scores(kv_cache[request][:, :, :head_size], mean_q[request], cov_q[request])
        every = every.reshape(lists, span, local_kv)
        picked = jnp.einsum("bjs,bsk->bkj", picker.astype(jnp.float32), every, precision=HIGHEST)
        block_kv.append(chosen)
        block_score.append(picked)
        block_count.append(jnp.sum((listed < span).astype(jnp.int32), axis=1))
    items_kv = jnp.concatenate(block_kv, axis=0)
    items_score = jnp.concatenate(block_score, axis=0)
    items_count = jnp.concatenate(block_count, axis=0)
    total_items = requests * lists
    targets = block_target.reshape(total_items, 2)
    offset = (targets[:, 0] - position) % ctx_count
    slot = targets[:, 1].reshape(requests, lists)
    peers = jnp.arange(ctx_count, dtype=jnp.int32)
    outgoing = targets[:, 0][None, :] == peers[:, None]
    send_kv = jnp.einsum(
        "pm,mjkc->pjkc", outgoing.astype(jnp.bfloat16), items_kv, preferred_element_type=jnp.float32
    ).astype(jnp.bfloat16)
    send_score = jnp.einsum(
        "pm,mkj->pkj", outgoing.astype(jnp.float32), items_score, precision=HIGHEST
    )
    send_count = jnp.sum(jnp.where(outgoing, items_count[None, :], 0), axis=1)
    recv_kv, recv_score, recv_count = (
        lax.all_to_all(send_kv, "ctx", split_axis=0, concat_axis=0, tiled=True),
        lax.all_to_all(
            send_score.astype(jnp.bfloat16), "ctx", split_axis=0, concat_axis=0, tiled=True
        ).astype(send_score.dtype),
        lax.all_to_all(send_count, "ctx", split_axis=0, concat_axis=0, tiled=True),
    )
    source = (position - offset) % ctx_count
    incoming = source[:, None] == peers[None, :]
    got_kv = jnp.einsum(
        "mp,pjkc->mjkc", incoming.astype(jnp.bfloat16), recv_kv, preferred_element_type=jnp.float32
    ).astype(jnp.bfloat16)
    got_score = jnp.einsum(
        "mp,pkj->mkj", incoming.astype(jnp.float32), recv_score, precision=HIGHEST
    )
    got_count = jnp.sum(jnp.where(incoming, recv_count[None, :], 0), axis=1)
    slot_table = slot[:, None, :] == jnp.arange(lists, dtype=jnp.int32)[None, :, None]
    placed_kv = jnp.einsum(
        "rsb,rbjkc->rsjkc",
        slot_table.astype(jnp.bfloat16),
        got_kv.reshape(requests, lists, width, local_kv, pair),
        preferred_element_type=jnp.float32,
    ).astype(jnp.bfloat16)
    packed_cache = placed_kv.reshape(requests, lists * width, local_kv, pair)
    placed_score = jnp.einsum(
        "rsb,rbkj->rksj",
        slot_table.astype(jnp.float32),
        got_score.reshape(requests, lists, local_kv, width),
        precision=HIGHEST,
    )
    packed_scores = placed_score.reshape(requests, local_kv, lists * width)
    placed_count = jnp.sum(jnp.where(slot_table, got_count.reshape(requests, 1, lists), 0), axis=2)
    live = (jnp.arange(width, dtype=jnp.int32)[None, None, :] < placed_count[:, :, None]).reshape(
        requests, lists * width
    )
    steps = new_tokens.shape[0]
    local_width = new_tokens.shape[2]
    flat = new_tokens.reshape(steps * requests, local_width)
    wide = flat.astype(jnp.float32)
    squares = jnp.sum(wide * wide, axis=1)
    query_part = jnp.dot(flat, w_query, preferred_element_type=jnp.float32)
    pair_part = jnp.dot(
        flat, w_keyval.reshape(local_width, local_kv * pair), preferred_element_type=jnp.float32
    )
    squares, query_part, pair_part = lax.psum((squares, query_part, pair_part), "ctx")
    inverse = lax.rsqrt(squares / D + EPSILON)
    query = (
        (query_part * inverse[:, None])
        .astype(jnp.bfloat16)
        .reshape(steps, requests, local_kv, group, head_size)
    )
    fresh = (
        (pair_part * inverse[:, None]).astype(jnp.bfloat16).reshape(steps, requests, local_kv, pair)
    )
    query = jnp.transpose(query, (1, 2, 0, 3, 4)).reshape(
        requests, local_kv, steps * group, head_size
    )
    fresh = jnp.transpose(fresh, (1, 2, 0, 3))
    logits = (
        jnp.einsum(
            "rkqd,rnkd->rkqn",
            query,
            packed_cache[..., :head_size],
            preferred_element_type=jnp.float32,
        )
        / root_size
    )
    logits = jnp.where(live[:, None, None, :], logits, -jnp.inf)
    top = jnp.max(logits, axis=3)
    weights = jnp.exp(logits - top[..., None])
    totals = jnp.sum(weights, axis=3)
    weighted = jnp.einsum(
        "rkqn,rnkd->rkqd",
        weights.astype(jnp.bfloat16),
        packed_cache[..., head_size:],
        preferred_element_type=jnp.float32,
    )
    top, totals, weighted = joined((top, totals, weighted), "ctx", combine_parts)
    recent = (
        jnp.einsum(
            "rkqd,rkud->rkqu", query, fresh[..., :head_size], preferred_element_type=jnp.float32
        )
        / root_size
    )
    causal = (jnp.arange(steps * group, dtype=jnp.int32) // group)[:, None] >= jnp.arange(
        steps, dtype=jnp.int32
    )[None, :]
    recent = jnp.where(causal[None, None], recent, -jnp.inf)
    best = jnp.maximum(top, jnp.max(recent, axis=3))
    weight_new = jnp.exp(recent - best[..., None])
    factor_old = jnp.exp(top - best)
    normalizer = totals * factor_old + jnp.sum(weight_new, axis=3)
    weighted = weighted * factor_old[..., None] + jnp.einsum(
        "rkqu,rkud->rkqd",
        weight_new.astype(jnp.bfloat16),
        fresh[..., head_size:],
        preferred_element_type=jnp.float32,
    )
    attended = (weighted / normalizer[..., None]).astype(jnp.bfloat16)
    attended = attended.reshape(requests, local_kv, steps, group, head_size)
    attended = jnp.transpose(attended, (2, 0, 1, 3, 4)).reshape(
        steps * requests, local_kv * group * head_size
    )
    partial_value = jnp.dot(attended, w_out, preferred_element_type=jnp.float32)
    summed_out = lax.psum(partial_value, "head")
    decoded = summed_out.astype(jnp.bfloat16).reshape(steps, requests, local_width)
    return (packed_cache, packed_scores, decoded)


def solution(mesh):
    in_specs = (
        P(None, "ctx", "head", None),
        P(None, "ctx", None),
        P(None, "ctx", None),
        P(None, "ctx", "head"),
        P(None, None, "ctx"),
        P("ctx", "head"),
        P("ctx", "head", None),
        P("head", "ctx"),
    )
    out_specs = (P(None, "ctx", "head", None), P(None, "head", "ctx"), P(None, None, "ctx"))
    body = sixteen if mesh.shape["ctx"] == 16 and mesh.shape["head"] == 2 else per_device
    return jax.shard_map(
        body, mesh=mesh, in_specs=in_specs, out_specs=out_specs, check_vma=False
    )
```
